256 devices in a mesh: row: 8 (over y, x_hi), col: 32 (over x_lo, z, core).
Axes of the slice: x: 4 (x_hi: 2, x_lo: 2; x = x_hi * 2 + x_lo), y: 4, z: 8, core: 2. Of those that a mesh axis runs over, the one named last changes fastest.
Arguments:
- queries: bfloat16 [64, 512, 512], P('row', 'col'), may hold values from -6 to 6
- keys: bfloat16 [64, 512, 512], P('row', 'col'), may hold values from -6 to 6
- values: bfloat16 [64, 512, 512], P('row', 'col'), may hold values from -6 to 6
- grad_out: bfloat16 [64, 512, 512], P('row', 'col'), may hold values from -6 to 6
- rel_bias: float32 [8, 17, 17], replicated, may hold values from -4 to 4
- occupied: int32 [8, 32], replicated, may hold values 0 or 1
Outputs:
- grad_queries: bfloat16 [64, 512, 512], P('row', 'col')
- grad_keys: bfloat16 [64, 512, 512], P('row', 'col')
- grad_values: bfloat16 [64, 512, 512], P('row', 'col')
- grad_bias: float32 [8, 17, 17], replicated
The draws below stay inside these ranges and needn't reach their ends.
All inputs are finite; a program needn't handle non-finite values.
Results may differ from the reference program's by a relative error of at most 0.015.
Values may be sent and summed in bfloat16 or wider, within the bound.
No kernel may reach another device: no remote copies, remote signals or barrier semaphores. Data moves between devices by JAX's collectives and lax.ppermute only.
A program may use at most 64 MiB of HBM per device.

```python
import jax
import jax.numpy as jnp
from jax import lax

HEADS = 8
HEAD_DIM = 64
WIDTH = 512
RAD = 8
WIN = 17
TR = 8
TC = 16
GRID_ROWS = 8
GRID_COLS = 32
NR = 64
NC = 512


def base_draw(key, fold_value):
    values = jax.random.normal(jax.random.fold_in(key, fold_value), (NR, NC, WIDTH), jnp.float32)
    return jnp.clip(values, -6.0, 6.0)


def draw_queries(key, part):
    values = base_draw(key, 3)
    return values.astype(jnp.bfloat16)


def draw_keys(key, part):
    values = base_draw(key, 5)
    return values.astype(jnp.bfloat16)


def plant(array, own_key, low, top_value):
    dims = array.shape
    index_at = [jax.random.randint(jax.random.fold_in(own_key, axis), (), 0, dims[axis]) for axis in range(len(dims))]
    array = array.at[tuple(index_at)].set(low)
    longest = dims.index(max(dims))
    index_at[longest] = (index_at[longest] + 1) % dims[longest]
    return array.at[tuple(index_at)].set(top_value)


def block_scale(stream_key, shape, split, smallest, largest):
    loudness, own = 1.0, jax.random.fold_in(stream_key, 6)
    for axis_at, blocks in split:
        steps = jnp.exp(jax.random.uniform(jax.random.fold_in(own, axis_at), (blocks,), jnp.float32, smallest / len(split), largest / len(split)))
        loudness = loudness * jnp.repeat(steps, shape[axis_at] // blocks).reshape([-1 if axis == axis_at else 1 for axis in range(len(shape))])
    return loudness


def scatter_about(own_key, dims, scale, most, cuts=(), held_as=jnp.bfloat16):
    array = scale * jax.random.normal(own_key, dims, jnp.float32)
    if cuts:
        array = array * block_scale(own_key, dims, cuts, -0.22, 0.18)
    return jnp.clip(array, -most, most).astype(held_as)


def setup_inputs(seed: int = 0) -> dict:
    splits = jax.random.split(jax.random.key(seed), 7)
    return {
        "queries": draw_queries(jax.random.fold_in(splits[6], 71), 0),
        "keys": draw_keys(jax.random.fold_in(splits[6], 71), 0),
        "values": scatter_about(splits[2], (NR, NC, WIDTH), 1.0, 6.0, ((0, 8), (1, 32))),
        "grad_out": scatter_about(splits[3], (NR, NC, WIDTH), 1.0, 6.0, ((0, 8), (1, 32))),
        "rel_bias": scatter_about(splits[4], (HEADS, WIN, WIN), 1.0, 4.0, (), jnp.float32),
        "occupied": plant((jax.random.randint(splits[5], (GRID_ROWS, GRID_COLS), 0, 4) < 3).astype(jnp.int32), jax.random.fold_in(splits[5], 1), 0, 1),
    }


def take_cells(padded, row_shift, col_shift):
    return lax.dynamic_slice(padded, (row_shift, col_shift, jnp.int32(0)), (NR, NC, padded.shape[2]))


def take_plane(padded, row_shift, col_shift):
    return lax.dynamic_slice(padded, (row_shift, col_shift), (NR, NC))


def reference(queries, keys, values, grad_out, rel_bias, occupied):
    score_scale = HEAD_DIM ** -0.5
    filled = jnp.repeat(jnp.repeat(occupied, TR, axis=0), TC, axis=1) > 0
    filled_pad = jnp.pad(filled, RAD)
    offsets = jnp.arange(WIN * WIN, dtype=jnp.int32)
    pad_spec = ((RAD, RAD), (RAD, RAD), (0, 0))

    def split_heads(stacked):
        return jnp.transpose(stacked.astype(jnp.float32).reshape(NR, NC, HEADS, HEAD_DIM), (2, 0, 1, 3))

    def one_head(packed):
        head_query, head_key, head_value, head_grad, head_bias = packed
        key_pad = jnp.pad(head_key, pad_spec)
        value_pad = jnp.pad(head_value, pad_spec)
        flat_bias = head_bias.reshape(WIN * WIN)

        def pair_terms(offset):
            row_shift = (offset // WIN).astype(jnp.int32)
            col_shift = (offset % WIN).astype(jnp.int32)
            usable = take_plane(filled_pad, row_shift, col_shift) & filled
            scores = jnp.sum(head_query * take_cells(key_pad, row_shift, col_shift), axis=-1) * score_scale + flat_bias[offset]
            grad_weights = jnp.sum(head_grad * take_cells(value_pad, row_shift, col_shift), axis=-1)
            return jnp.where(usable, scores, -jnp.inf), grad_weights, usable

        all_scores, all_grads, all_usable = lax.map(pair_terms, offsets)
        row_max = jnp.where(filled, jnp.max(all_scores, axis=0), 0.0)
        exponent = jnp.where(all_usable, jnp.exp(all_scores - row_max), 0.0)
        row_total = jnp.where(filled, jnp.sum(exponent, axis=0), 1.0)
        weights = exponent / row_total
        row_delta = jnp.sum(weights * all_grads, axis=0)
        grad_scores = weights * (all_grads - row_delta)
        grad_bias = jnp.sum(grad_scores, axis=(1, 2)).reshape(WIN, WIN)
        weights_low = lax.optimization_barrier(weights.astype(jnp.bfloat16)).astype(jnp.float32)
        grad_scores_low = lax.optimization_barrier(grad_scores.astype(jnp.bfloat16)).astype(jnp.float32)
        query_pad = jnp.pad(head_query, pad_spec)
        grad_pad = jnp.pad(head_grad, pad_spec)
        scores_pad = jnp.pad(grad_scores_low, ((0, 0), (RAD, RAD), (RAD, RAD)))
        weights_pad = jnp.pad(weights_low, ((0, 0), (RAD, RAD), (RAD, RAD)))

        def gather_grads(carried, offset):
            grad_query, grad_key, grad_value = carried
            row_shift = (offset // WIN).astype(jnp.int32)
            col_shift = (offset % WIN).astype(jnp.int32)
            back_row = (2 * RAD - row_shift).astype(jnp.int32)
            back_col = (2 * RAD - col_shift).astype(jnp.int32)
            grad_query = grad_query + grad_scores_low[offset][..., None] * take_cells(key_pad, row_shift, col_shift)
            grad_key = grad_key + take_plane(scores_pad[offset], back_row, back_col)[..., None] * take_cells(query_pad, back_row, back_col)
            grad_value = grad_value + take_plane(weights_pad[offset], back_row, back_col)[..., None] * take_cells(grad_pad, back_row, back_col)
            return (grad_query, grad_key, grad_value), None

        initial = jnp.zeros((NR, NC, HEAD_DIM), jnp.float32)
        (grad_query, grad_key, grad_value), _ = lax.scan(gather_grads, (initial, initial, initial), offsets)
        return grad_query * score_scale, grad_key * score_scale, grad_value, grad_bias

    all_query, all_key, all_value, all_bias = lax.map(
        one_head, (split_heads(queries), split_heads(keys), split_heads(values), split_heads(grad_out), rel_bias))

    def merge_heads(stacked):
        return jnp.transpose(stacked, (1, 2, 0, 3)).reshape(NR, NC, HEADS * HEAD_DIM).astype(jnp.bfloat16)

    return merge_heads(all_query), merge_heads(all_key), merge_heads(all_value), all_bias
```

```python
import functools

import jax
import jax.numpy as jnp
from jax import lax
from jax.experimental import pallas as pl
from jax.experimental.pallas import tpu as pltpu
from jax.sharding import PartitionSpec as P

LOG2E = 1.4426950408889634
MASKED = -1e30
VMEM_SPEC = pl.BlockSpec(memory_space=pltpu.VMEM)
SMEM_SPEC = pl.BlockSpec(memory_space=pltpu.SMEM)


def lanes_of(shape):
    return lax.broadcasted_iota(jnp.int32, shape, len(shape) - 1)


def swap_halves(array):
    return pltpu.roll(array, 64, 1)


def pack_kernel(q_ref, k_ref, v_ref, g_ref, out_ref):
    low = lanes_of((128, 128)) < 64
    for pair in range(4):
        lanes = pl.ds(128 * pair, 128)

        def load(ref):
            return ref[:, :, lanes].astype(jnp.float32)

        def by_halves(block):
            split = block.reshape(8, 2, 8, 128)
            return jnp.concatenate(
                [split[:, half].reshape(64, 128) for half in range(2)], axis=0
            )

        query = load(q_ref).reshape(128, 128) * 0.125
        grad = load(g_ref).reshape(128, 128)
        key = by_halves(load(k_ref))
        value = by_halves(load(v_ref))
        for at, first, second in ((0, query, grad), (128, key, value)):
            even = jnp.where(low, first, swap_halves(second))
            odd = jnp.where(low, swap_halves(first), second)
            out_ref[2 * pair, at : at + 128, :] = even.astype(jnp.bfloat16)
            out_ref[2 * pair + 1, at : at + 128, :] = odd.astype(jnp.bfloat16)


def pack(queries, keys, values, grad_out):
    return pl.pallas_call(
        pack_kernel,
        out_shape=jax.ShapeDtypeStruct((8, 256, 128), jnp.bfloat16),
        in_specs=[VMEM_SPEC] * 4,
        out_specs=VMEM_SPEC,
        name="pack",
    )(queries, keys, values, grad_out)


def build_table(head, bias_ref, rows_ref, table_ref):
    lane = lanes_of((544, 128))
    sub = lax.broadcasted_iota(jnp.int32, (544, 128), 0)
    rows_ref[...] = jnp.zeros_like(rows_ref)
    for a in range(17):
        rows_ref[a : a + 1, 0:17] = bias_ref[a, pl.ds(head, 1), :]
    spread = jnp.concatenate(
        [jnp.broadcast_to(rows_ref[a : a + 1, :], (32, 128)) for a in range(17)], axis=0
    )
    b_index = sub & 31
    column = jnp.sum(jnp.where(lane == b_index, spread, 0.0), axis=1, keepdims=True)
    skewed = jnp.where(b_index < 17, column * LOG2E, MASKED)
    query_col = lane & 15
    for bit in (1, 2, 4, 8):
        skewed = jnp.where((query_col & bit) > 0, pltpu.roll(skewed, bit, 0), skewed)
    blocks = skewed.reshape(17, 32, 128)
    empty = jnp.full((7, 32, 128), MASKED, jnp.float32)
    padded = jnp.concatenate([empty, blocks, empty], axis=0)
    query_row = lanes_of((24, 32, 128)) >> 4
    table = padded[7:31]
    for row in range(1, 8):
        table = jnp.where(query_row == row, padded[7 - row : 31 - row], table)
    table = table.reshape(3, 8, 4, 8, 128)
    for chunk in range(4):
        table_ref[:, chunk] = table[:, :, chunk]


def contract_bias(sums_ref, skew_ref, bias_out_ref):
    query_row = lanes_of((17, 8, 128)) >> 4
    for chunk in range(4):
        by_row = sums_ref[:, chunk].reshape(24, 8, 128)
        picked = by_row[0:17]
        for row in range(1, 8):
            picked = jnp.where(query_row == row, by_row[row : row + 17], picked)
        skew_ref[:, chunk] = picked
    skewed = skew_ref[...].reshape(544, 128)
    query_col = lanes_of((544, 128)) & 15
    for bit in (1, 2, 4, 8):
        skewed = jnp.where((query_col & bit) > 0, pltpu.roll(skewed, 544 - bit, 0), skewed)
    skewed = jnp.concatenate([skewed, jnp.zeros((96, 128), jnp.float32)], axis=0)
    total = lax.dot_general(
        jnp.ones((8, 128), jnp.float32),
        skewed,
        (((1,), (1,)), ((), ())),
        precision=lax.Precision.HIGHEST,
        preferred_element_type=jnp.float32,
    )
    rows = [total[0:1, 128 * k : 128 * k + 128] for k in range(5)]
    rows.append(jnp.zeros((3, 128), jnp.float32))
    block = jnp.concatenate(rows, axis=0)
    bias_out_ref[...] = jnp.broadcast_to(block[None], bias_out_ref.shape)


def main_kernel(
    occ_ref,
    bias_ref,
    x_ref,
    left_ref,
    right_ref,
    dq_ref,
    own_ref,
    out_left_ref,
    out_right_ref,
    bias_out_ref,
    rows_ref,
    table_ref,
    sums_ref,
    skew_ref,
    kv_ref,
    kt_ref,
    qg_ref,
    p_ref,
):
    head = lax.axis_index("row")
    col = lax.axis_index("col")
    col_count = occ_ref.shape[1]
    build_table(head, bias_ref, rows_ref, table_ref)
    sums_ref[...] = jnp.zeros_like(sums_ref)
    for edge in (0, 9):
        kv_ref[edge] = jnp.zeros((256, 128), jnp.bfloat16)
        kt_ref[edge] = jnp.zeros((128, 256), jnp.bfloat16)
        qg_ref[edge] = jnp.zeros((256, 128), jnp.bfloat16)
    p_ref[1, :, 0:256] = jnp.zeros((256, 256), jnp.bfloat16)
    p_ref[8, :, 512:768] = jnp.zeros((256, 256), jnp.bfloat16)
    low = lanes_of((128, 128)) < 64

    def stage(j, carry):
        kv_ref[j + 1, 0:64] = left_ref[j]
        kv_ref[j + 1, 64:192] = x_ref[j, 128:256]
        kv_ref[j + 1, 192:256] = right_ref[j]
        kt_ref[j + 1] = jnp.transpose(kv_ref[j + 1].astype(jnp.float32)).astype(jnp.bfloat16)
        query_grad = x_ref[j, 0:128].astype(jnp.float32)
        qg_ref[j + 1, 0:128] = jnp.where(low, query_grad, 0.0).astype(jnp.bfloat16)
        qg_ref[j + 1, 128:256] = jnp.where(low, 0.0, query_grad).astype(jnp.bfloat16)
        return carry

    lax.fori_loop(0, 8, stage, 0)

    def filled(row, at):
        inside = (row >= 0) & (row < 8) & (at >= 0) & (at < col_count)
        value = occ_ref[jnp.clip(row, 0, 7), jnp.clip(at, 0, col_count - 1)]
        return inside & (value > 0)

    def penalty(row, at):
        return jnp.where(filled(row, at), jnp.float32(0.0), jnp.float32(MASKED))

    def tile(i, carry):
        keys = kv_ref[pl.ds(i, 3)].reshape(768, 128)
        both = lax.dot_general(
            keys, qg_ref[i + 1], (((1,), (1,)), ((), ())), preferred_element_type=jnp.float32
        )
        scores, grads = both[:, 0:128], both[:, 128:256]
        shifted = []
        for step in range(3):
            row = i - 1 + step
            own = penalty(row, col)
            marks = (penalty(row, col - 1), own, own, penalty(row, col + 1))
            for chunk in range(4):
                at = 256 * step + 64 * chunk
                bias = table_ref[step, chunk].reshape(64, 128)
                shifted.append(scores[at : at + 64] * LOG2E + (bias + marks[chunk]))
        shifted = jnp.concatenate(shifted, axis=0)
        top = jnp.max(shifted, axis=0, keepdims=True)
        exponent = jnp.exp2(shifted - top)
        total = jnp.sum(exponent, axis=0, keepdims=True)
        weighted = jnp.sum(exponent * grads, axis=0, keepdims=True)
        inverse = 1.0 / total
        delta = weighted * inverse
        used = jnp.where(filled(i, col), jnp.float32(1.0), jnp.float32(0.0))
        weights = exponent * (inverse * used)
        grad_scores = weights * (grads - delta)
        sums_ref[...] += grad_scores.reshape(3, 4, 8, 8, 128)
        weights_low = weights.astype(jnp.bfloat16)
        grad_low = grad_scores.astype(jnp.bfloat16)
        grad_query = jnp.zeros((128, 128), jnp.float32)
        for step in range(3):
            part = grad_low[256 * step : 256 * step + 256]
            slot = 256 * (2 - step)
            p_ref[i + step, :, slot : slot + 128] = part
            p_ref[i + step, :, slot + 128 : slot + 256] = weights_low[256 * step : 256 * step + 256]
            grad_query += jnp.dot(kt_ref[i + step], part, preferred_element_type=jnp.float32)
        grad_query = jnp.transpose(grad_query * 0.125)
        packed = jnp.where(low[0:64], grad_query[0:64], swap_halves(grad_query[64:128]))
        dq_ref[i] = packed.astype(jnp.bfloat16)
        return carry

    lax.fori_loop(0, 8, tile, 0)

    def keys_pass(j, carry):
        result = jnp.dot(
            p_ref[j + 1],
            qg_ref[pl.ds(j, 3)].reshape(768, 128),
            preferred_element_type=jnp.float32,
        )
        out_left_ref[j] = result[0:64].astype(jnp.bfloat16)
        own_ref[j] = result[64:192]
        out_right_ref[j] = result[192:256].astype(jnp.bfloat16)
        return carry

    lax.fori_loop(0, 8, keys_pass, 0)
    contract_bias(sums_ref, skew_ref, bias_out_ref)


def main(occupied, bias, blocks, left, right, col_count):
    halo = jax.ShapeDtypeStruct((8, 64, 128), jnp.bfloat16)
    return pl.pallas_call(
        main_kernel,
        out_shape=(
            halo,
            jax.ShapeDtypeStruct((8, 128, 128), jnp.float32),
            halo,
            halo,
            jax.ShapeDtypeStruct((col_count, 8, 128), jnp.float32),
        ),
        in_specs=[SMEM_SPEC] + [VMEM_SPEC] * 4,
        out_specs=(VMEM_SPEC,) * 5,
        scratch_shapes=[
            pltpu.VMEM((24, 128), jnp.float32),
            pltpu.VMEM((3, 4, 8, 8, 128), jnp.float32),
            pltpu.VMEM((3, 4, 8, 8, 128), jnp.float32),
            pltpu.VMEM((17, 4, 8, 128), jnp.float32),
            pltpu.VMEM((10, 256, 128), jnp.bfloat16),
            pltpu.VMEM((10, 128, 256), jnp.bfloat16),
            pltpu.VMEM((10, 256, 128), jnp.bfloat16),
            pltpu.VMEM((10, 256, 768), jnp.bfloat16),
        ],
        compiler_params=pltpu.CompilerParams(vmem_limit_bytes=40 << 20),
        name="attention_backward",
    )(occupied, bias, blocks, left, right)


def combine_kernel(dq_ref, own_ref, left_ref, right_ref, bias_ref, out_ref):
    total = jnp.sum(bias_ref[...], axis=0)
    high = total.astype(jnp.bfloat16).astype(jnp.float32)
    rest = total - high
    middle = rest.astype(jnp.bfloat16).astype(jnp.float32)
    pieces = jnp.concatenate([high, middle, rest - middle, jnp.zeros_like(total)], axis=0)
    pieces = pieces.astype(jnp.bfloat16)
    for i in range(8):
        out_ref[i, 0:64] = dq_ref[i]
        for at, ref in ((0, left_ref), (64, right_ref)):
            summed = own_ref[i, at : at + 64] + ref[i].astype(jnp.float32)
            out_ref[i, 64 + at : 128 + at] = summed.astype(jnp.bfloat16)
        out_ref[i, 192:224] = pieces


def combine(dq, own, left, right, bias):
    return pl.pallas_call(
        combine_kernel,
        out_shape=jax.ShapeDtypeStruct((8, 224, 128), jnp.bfloat16),
        in_specs=[VMEM_SPEC] * 5,
        out_specs=VMEM_SPEC,
        name="combine",
    )(dq, own, left, right, bias)


def unpack_kernel(z_ref, gq_ref, gk_ref, gv_ref, gb_ref, bias_ref):
    low = lanes_of((128, 128)) < 64

    def by_rows(block):
        split = block.reshape(2, 8, 8, 128)
        return jnp.concatenate([split[0], split[1]], axis=1)

    for pair in range(4):
        lanes = pl.ds(128 * pair, 128)
        even = z_ref[2 * pair].astype(jnp.float32)
        odd = z_ref[2 * pair + 1].astype(jnp.float32)
        first = jnp.where(low[0:64], even[0:64], swap_halves(odd[0:64]))
        second = jnp.where(low[0:64], swap_halves(even[0:64]), odd[0:64])
        query = jnp.concatenate([first, second], axis=0)
        gq_ref[:, :, lanes] = query.reshape(8, 16, 128).astype(jnp.bfloat16)
        key = jnp.where(low, even[64:192], swap_halves(odd[64:192]))
        value = jnp.where(low, swap_halves(even[64:192]), odd[64:192])
        gk_ref[:, :, lanes] = by_rows(key).astype(jnp.bfloat16)
        gv_ref[:, :, lanes] = by_rows(value).astype(jnp.bfloat16)
        for head, block in ((2 * pair, even), (2 * pair + 1, odd)):
            bias_ref[head] = block[192:200] + block[200:208] + block[208:216]
    for a in range(17):
        row = bias_ref[:, a // 4, :]
        if a % 4:
            row = pltpu.roll(row, 128 - 32 * (a % 4), 1)
        gb_ref[a] = row[:, 0:17]


def unpack(blocks):
    token = jax.ShapeDtypeStruct((8, 16, 512), jnp.bfloat16)
    return pl.pallas_call(
        unpack_kernel,
        out_shape=(token, token, token, jax.ShapeDtypeStruct((17, 8, 17), jnp.float32)),
        in_specs=[VMEM_SPEC],
        out_specs=(VMEM_SPEC,) * 4,
        scratch_shapes=[pltpu.VMEM((8, 8, 128), jnp.float32)],
        name="unpack",
    )(blocks)


def shards(queries, keys, values, grad_out, rel_bias, occupied):
    col_count = lax.axis_size("col")
    rightward = [(i, i + 1) for i in range(col_count - 1)]
    leftward = [(i + 1, i) for i in range(col_count - 1)]
    packed = pack(queries, keys, values, grad_out)
    blocks = lax.all_to_all(packed, "row", 0, 0)
    from_left = lax.ppermute(blocks[:, 192:256], "col", rightward)
    from_right = lax.ppermute(blocks[:, 128:192], "col", leftward)
    bias = jnp.transpose(rel_bias, (1, 0, 2))
    dq, own, out_left, out_right, bias_part = main(
        occupied, bias, blocks, from_left, from_right, col_count
    )
    share_left = lax.ppermute(out_right, "col", rightward)
    share_right = lax.ppermute(out_left, "col", leftward)
    bias_parts = lax.all_to_all(bias_part, "col", 0, 0)
    returned = lax.all_to_all(combine(dq, own, share_left, share_right, bias_parts), "row", 0, 0)
    grad_query, grad_key, grad_value, grad_bias = unpack(returned)
    return grad_query, grad_key, grad_value, jnp.transpose(grad_bias, (1, 0, 2))


def solution(mesh):
    token = P("row", "col", None)
    return jax.shard_map(
        shards,
        mesh=mesh,
        in_specs=(token, token, token, token, P(), P()),
        out_specs=(token, token, token, P()),
        check_vma=False,
    )
```

```python
import functools

import jax
import jax.numpy as jnp
from jax import lax
from jax.experimental import pallas as pl
from jax.experimental.pallas import tpu as pltpu
from jax.sharding import PartitionSpec as P

LOG2E = 1.4426950408889634
MASKED = -1e30
VMEM_SPEC = pl.BlockSpec(memory_space=pltpu.VMEM)
SMEM_SPEC = pl.BlockSpec(memory_space=pltpu.SMEM)


def lanes_of(shape):
    return lax.broadcasted_iota(jnp.int32, shape, len(shape) - 1)


def swap_halves(array):
    return pltpu.roll(array, 64, 1)


def pack_kernel(q_ref, k_ref, v_ref, g_ref, out_ref):
    low = lanes_of((128, 128)) < 64
    for pair in range(4):
        lanes = pl.ds(128 * pair, 128)

        def load(ref):
            return ref[:, :, lanes].astype(jnp.float32)

        def by_halves(block):
            split = block.reshape(8, 2, 8, 128)
            return jnp.concatenate(
                [split[:, half].reshape(64, 128) for half in range(2)], axis=0
            )

        query = load(q_ref).reshape(128, 128) * 0.125
        grad = load(g_ref).reshape(128, 128)
        key = by_halves(load(k_ref))
        value = by_halves(load(v_ref))
        for at, first, second in ((0, query, grad), (128, key, value)):
            even = jnp.where(low, first, swap_halves(second))
            odd = jnp.where(low, swap_halves(first), second)
            out_ref[2 * pair, at : at + 128, :] = even.astype(jnp.bfloat16)
            out_ref[2 * pair + 1, at : at + 128, :] = odd.astype(jnp.bfloat16)


def pack(queries, keys, values, grad_out):
    return pl.pallas_call(
        pack_kernel,
        out_shape=jax.ShapeDtypeStruct((8, 256, 128), jnp.bfloat16),
        in_specs=[VMEM_SPEC] * 4,
        out_specs=VMEM_SPEC,
        name="pack",
    )(queries, keys, values, grad_out)


def build_table(head, bias_ref, rows_ref, table_ref):
    lane = lanes_of((544, 128))
    sub = lax.broadcasted_iota(jnp.int32, (544, 128), 0)
    rows_ref[...] = jnp.zeros_like(rows_ref)
    for a in range(17):
        rows_ref[a : a + 1, 0:17] = bias_ref[a, pl.ds(head, 1), :]
    spread = jnp.concatenate(
        [jnp.broadcast_to(rows_ref[a : a + 1, :], (32, 128)) for a in range(17)], axis=0
    )
    b_index = sub & 31
    column = jnp.sum(jnp.where(lane == b_index, spread, 0.0), axis=1, keepdims=True)
    skewed = jnp.where(b_index < 17, column * LOG2E, MASKED)
    query_col = lane & 15
    for bit in (1, 2, 4, 8):
        skewed = jnp.where((query_col & bit) > 0, pltpu.roll(skewed, bit, 0), skewed)
    blocks = skewed.reshape(17, 32, 128)
    empty = jnp.full((7, 32, 128), MASKED, jnp.float32)
    padded = jnp.concatenate([empty, blocks, empty], axis=0)
    query_row = lanes_of((24, 32, 128)) >> 4
    table = padded[7:31]
    for row in range(1, 8):
        table = jnp.where(query_row == row, padded[7 - row : 31 - row], table)
    table = table.reshape(3, 8, 4, 8, 128)
    for chunk in range(4):
        table_ref[:, chunk] = table[:, :, chunk]


def contract_bias(sums_ref, skew_ref, bias_out_ref):
    query_row = lanes_of((17, 8, 128)) >> 4
    for chunk in range(4):
        by_row = sums_ref[:, chunk].reshape(24, 8, 128)
        picked = by_row[0:17]
        for row in range(1, 8):
            picked = jnp.where(query_row == row, by_row[row : row + 17], picked)
        skew_ref[:, chunk] = picked
    skewed = skew_ref[...].reshape(544, 128)
    query_col = lanes_of((544, 128)) & 15
    for bit in (1, 2, 4, 8):
        skewed = jnp.where((query_col & bit) > 0, pltpu.roll(skewed, 544 - bit, 0), skewed)
    skewed = jnp.concatenate([skewed, jnp.zeros((96, 128), jnp.float32)], axis=0)
    total = lax.dot_general(
        jnp.ones((8, 128), jnp.float32),
        skewed,
        (((1,), (1,)), ((), ())),
        precision=lax.Precision.HIGHEST,
        preferred_element_type=jnp.float32,
    )
    rows = [total[0:1, 128 * k : 128 * k + 128] for k in range(5)]
    rows.append(jnp.zeros((3, 128), jnp.float32))
    block = jnp.concatenate(rows, axis=0)
    bias_out_ref[...] = jnp.broadcast_to(block[None], bias_out_ref.shape)


def main_kernel(
    occ_ref,
    bias_ref,
    x_ref,
    left_ref,
    right_ref,
    dq_ref,
    own_ref,
    out_left_ref,
    out_right_ref,
    bias_out_ref,
    rows_ref,
    table_ref,
    sums_ref,
    skew_ref,
    kv_ref,
    kt_ref,
    qg_ref,
    p_ref,
):
    head = lax.axis_index("row")
    col = lax.axis_index("col")
    col_count = occ_ref.shape[1]
    build_table(head, bias_ref, rows_ref, table_ref)
    low = lanes_of((128, 128)) < 64
    sums_ref[...] = jnp.zeros_like(sums_ref)

    def filled(row, at):
        inside = (at >= 0) & (at < col_count)
        return inside & (occ_ref[row, jnp.clip(at, 0, col_count - 1)] > 0)

    def penalty(row, at):
        return jnp.where(filled(row, at), jnp.float32(0.0), jnp.float32(MASKED))

    marks = []
    for j in range(8):
        kv_ref[256 * j : 256 * j + 64] = left_ref[j]
        kv_ref[256 * j + 64 : 256 * j + 192] = x_ref[j, 128:256]
        kv_ref[256 * j + 192 : 256 * j + 256] = right_ref[j]
        flipped = jnp.transpose(kv_ref[256 * j : 256 * j + 256])
        kt_ref[:, 256 * j : 256 * j + 256] = flipped[0:64]
        query_grad = x_ref[j, 0:128]
        zero = jnp.zeros_like(query_grad)
        qg_ref[256 * j : 256 * j + 128] = jnp.where(low, query_grad, zero)
        qg_ref[256 * j + 128 : 256 * j + 256] = jnp.where(low, zero, query_grad)
        own = penalty(j, col)
        marks.append((penalty(j, col - 1), own, own, penalty(j, col + 1)))

    def window(i):
        steps = [step for step in range(3) if 0 <= i - 1 + step < 8]
        return steps, i - 1 + steps[0], len(steps)

    def products(i):
        _, first, count = window(i)
        return lax.dot_general(
            kv_ref[256 * first : 256 * (first + count)],
            qg_ref[256 * i : 256 * i + 256],
            (((1,), (1,)), ((), ())),
            preferred_element_type=jnp.float32,
        )

    def softmax(i, both):
        steps, first, count = window(i)
        scores, grads = both[:, 0:128], both[:, 128:256]
        shifted = []
        for step in steps:
            for chunk in range(4):
                at = 256 * (step - steps[0]) + 64 * chunk
                bias = table_ref[step, chunk].reshape(64, 128) + marks[i - 1 + step][chunk]
                shifted.append(scores[at : at + 64] * LOG2E + bias)
        shifted = jnp.concatenate(shifted, axis=0)
        top = jnp.max(shifted, axis=0, keepdims=True)
        exponent = jnp.exp2(shifted - top)
        total = jnp.sum(exponent, axis=0, keepdims=True)
        weighted = jnp.sum(exponent * grads, axis=0, keepdims=True)
        inverse = 1.0 / total
        delta = weighted * inverse
        used = jnp.where(filled(i, col), jnp.float32(1.0), jnp.float32(0.0))
        weights = exponent * (inverse * used)
        grad_scores = weights * (grads - delta)
        sums_ref[steps[0] : steps[-1] + 1] += grad_scores.reshape(count, 4, 8, 8, 128)
        return weights.astype(jnp.bfloat16), grad_scores.astype(jnp.bfloat16)

    def gradients(i, weights_low, grad_low):
        steps, first, count = window(i)
        shares = jnp.dot(
            jnp.concatenate([grad_low, weights_low], axis=1),
            qg_ref[256 * i : 256 * i + 256],
            preferred_element_type=jnp.float32,
        )
        grad_query = jnp.dot(
            kt_ref[:, 256 * first : 256 * (first + count)],
            grad_low,
            preferred_element_type=jnp.float32,
        )
        dq_ref[i] = (grad_query * 0.125).astype(jnp.bfloat16)
        for step in steps:
            at = 256 * (step - steps[0])
            j = i - 1 + step
            part = shares[at : at + 256]
            if not (step == 2 or i == 0):
                part = part + p_ref[j]
            if step == 0 or i == 7:
                out_left_ref[j] = part[0:64].astype(jnp.bfloat16)
                own_ref[j] = part[64:192]
                out_right_ref[j] = part[192:256].astype(jnp.bfloat16)
            else:
                p_ref[j] = part

    both = {i: products(i) for i in range(8)}
    pairs = [softmax(i, both[i]) for i in range(8)]
    for i in range(8):
        gradients(i, *pairs[i])
    contract_bias(sums_ref, skew_ref, bias_out_ref)


def main(occupied, bias, blocks, left, right, col_count):
    halo = jax.ShapeDtypeStruct((8, 64, 128), jnp.bfloat16)
    return pl.pallas_call(
        main_kernel,
        out_shape=(
            halo,
            jax.ShapeDtypeStruct((8, 128, 128), jnp.float32),
            halo,
            halo,
            jax.ShapeDtypeStruct((col_count, 8, 128), jnp.float32),
        ),
        in_specs=[SMEM_SPEC] + [VMEM_SPEC] * 4,
        out_specs=(VMEM_SPEC,) * 5,
        scratch_shapes=[
            pltpu.VMEM((24, 128), jnp.float32),
            pltpu.VMEM((3, 4, 8, 8, 128), jnp.float32),
            pltpu.VMEM((3, 4, 8, 8, 128), jnp.float32),
            pltpu.VMEM((17, 4, 8, 128), jnp.float32),
            pltpu.VMEM((2048, 128), jnp.bfloat16),
            pltpu.VMEM((64, 2048), jnp.bfloat16),
            pltpu.VMEM((2048, 128), jnp.bfloat16),
            pltpu.VMEM((8, 256, 128), jnp.float32),
        ],
        compiler_params=pltpu.CompilerParams(vmem_limit_bytes=40 << 20),
        name="attention_backward",
    )(occupied, bias, blocks, left, right)


def combine_kernel(dq_ref, own_ref, left_ref, right_ref, bias_ref, out_ref):
    total = jnp.sum(bias_ref[...], axis=0)
    high = total.astype(jnp.bfloat16).astype(jnp.float32)
    rest = total - high
    middle = rest.astype(jnp.bfloat16).astype(jnp.float32)
    pieces = jnp.concatenate([high, middle, rest - middle, jnp.zeros_like(total)], axis=0)
    pieces = pieces.astype(jnp.bfloat16)
    for i in range(8):
        out_ref[i, 0:64] = dq_ref[i]
        for at, ref in ((0, left_ref), (64, right_ref)):
            summed = own_ref[i, at : at + 64] + ref[i].astype(jnp.float32)
            out_ref[i, 64 + at : 128 + at] = summed.astype(jnp.bfloat16)
        out_ref[i, 192:224] = pieces


def combine(dq, own, left, right, bias):
    return pl.pallas_call(
        combine_kernel,
        out_shape=jax.ShapeDtypeStruct((8, 224, 128), jnp.bfloat16),
        in_specs=[VMEM_SPEC] * 5,
        out_specs=VMEM_SPEC,
        name="combine",
    )(dq, own, left, right, bias)


def unpack_kernel(z_ref, gq_ref, gk_ref, gv_ref, gb_ref, bias_ref):
    low = lanes_of((128, 128)) < 64

    def by_rows(block):
        split = block.reshape(2, 8, 8, 128)
        return jnp.concatenate([split[0], split[1]], axis=1)

    for pair in range(4):
        lanes = pl.ds(128 * pair, 128)
        even = z_ref[2 * pair].astype(jnp.float32)
        odd = z_ref[2 * pair + 1].astype(jnp.float32)
        query = jnp.transpose(jnp.concatenate([even[0:64], odd[0:64]], axis=0))
        gq_ref[:, :, lanes] = query.reshape(8, 16, 128).astype(jnp.bfloat16)
        key = jnp.where(low, even[64:192], swap_halves(odd[64:192]))
        value = jnp.where(low, swap_halves(even[64:192]), odd[64:192])
        gk_ref[:, :, lanes] = by_rows(key).astype(jnp.bfloat16)
        gv_ref[:, :, lanes] = by_rows(value).astype(jnp.bfloat16)
        for head, block in ((2 * pair, even), (2 * pair + 1, odd)):
            bias_ref[head] = block[192:200] + block[200:208] + block[208:216]
    for a in range(17):
        row = bias_ref[:, a // 4, :]
        if a % 4:
            row = pltpu.roll(row, 128 - 32 * (a % 4), 1)
        gb_ref[a] = row[:, 0:17]


def unpack(blocks):
    token = jax.ShapeDtypeStruct((8, 16, 512), jnp.bfloat16)
    return pl.pallas_call(
        unpack_kernel,
        out_shape=(token, token, token, jax.ShapeDtypeStruct((17, 8, 17), jnp.float32)),
        in_specs=[VMEM_SPEC],
        out_specs=(VMEM_SPEC,) * 4,
        scratch_shapes=[pltpu.VMEM((8, 8, 128), jnp.float32)],
        name="unpack",
    )(blocks)


def shards(queries, keys, values, grad_out, rel_bias, occupied):
    col_count = lax.axis_size("col")
    rightward = [(i, i + 1) for i in range(col_count - 1)]
    leftward = [(i + 1, i) for i in range(col_count - 1)]
    packed = pack(queries, keys, values, grad_out)
    blocks = lax.all_to_all(packed, "row", 0, 0)
    from_left = lax.ppermute(blocks[:, 192:256], "col", rightward)
    from_right = lax.ppermute(blocks[:, 128:192], "col", leftward)
    bias = jnp.transpose(rel_bias, (1, 0, 2))
    dq, own, out_left, out_right, bias_part = main(
        occupied, bias, blocks, from_left, from_right, col_count
    )
    share_left = lax.ppermute(out_right, "col", rightward)
    share_right = lax.ppermute(out_left, "col", leftward)
    bias_parts = lax.all_to_all(bias_part, "col", 0, 0)
    returned = lax.all_to_all(combine(dq, own, share_left, share_right, bias_parts), "row", 0, 0)
    grad_query, grad_key, grad_value, grad_bias = unpack(returned)
    return grad_query, grad_key, grad_value, jnp.transpose(grad_bias, (1, 0, 2))


def solution(mesh):
    token = P("row", "col", None)
    return jax.shard_map(
        shards,
        mesh=mesh,
        in_specs=(token, token, token, token, P(), P()),
        out_specs=(token, token, token, P()),
        check_vma=False,
    )
```

```python
import functools

import jax
import jax.numpy as jnp
from jax import lax
from jax.experimental import pallas as pl
from jax.experimental.pallas import tpu as pltpu
from jax.sharding import PartitionSpec as P

LOG2E = 1.4426950408889634
MASKED = -1e30
VMEM_SPEC = pl.BlockSpec(memory_space=pltpu.VMEM)
HBM_SPEC = pl.BlockSpec(memory_space=pltpu.HBM)
SMEM_SPEC = pl.BlockSpec(memory_space=pltpu.SMEM)


def lanes_of(shape):
    return lax.broadcasted_iota(jnp.int32, shape, len(shape) - 1)


def swap_halves(array):
    return pltpu.roll(array, 64, 1)


def pack_kernel(q_hbm, k_hbm, v_hbm, g_hbm, out_ref, q_ref, k_ref, v_ref, g_ref, sems):
    copies = [
        pltpu.make_async_copy(source, target, sems.at[at])
        for at, (source, target) in enumerate(
            ((q_hbm, q_ref), (g_hbm, g_ref), (k_hbm, k_ref), (v_hbm, v_ref))
        )
    ]
    for copy in copies:
        copy.start()
    for copy in copies:
        copy.wait()
    low = lanes_of((128, 128)) < 64
    for pair in range(4):
        lanes = pl.ds(128 * pair, 128)

        def load(ref):
            return ref[:, :, lanes].astype(jnp.float32)

        def by_halves(block):
            split = block.reshape(8, 2, 8, 128)
            return jnp.concatenate(
                [split[:, half].reshape(64, 128) for half in range(2)], axis=0
            )

        query = load(q_ref).reshape(128, 128) * 0.125
        grad = load(g_ref).reshape(128, 128)
        key = by_halves(load(k_ref))
        value = by_halves(load(v_ref))
        for at, first, second in ((0, query, grad), (128, key, value)):
            even = jnp.where(low, first, swap_halves(second))
            odd = jnp.where(low, swap_halves(first), second)
            out_ref[2 * pair, at : at + 128, :] = even.astype(jnp.bfloat16)
            out_ref[2 * pair + 1, at : at + 128, :] = odd.astype(jnp.bfloat16)


def pack(queries, keys, values, grad_out):
    return pl.pallas_call(
        pack_kernel,
        out_shape=jax.ShapeDtypeStruct((8, 256, 128), jnp.bfloat16),
        in_specs=[HBM_SPEC] * 4,
        out_specs=VMEM_SPEC,
        scratch_shapes=[pltpu.VMEM((8, 16, 512), jnp.bfloat16)] * 4
        + [pltpu.SemaphoreType.DMA((4,))],
        compiler_params=pltpu.CompilerParams(vmem_limit_bytes=60 << 20),
        name="pack",
    )(queries, keys, values, grad_out)


def build_table(head, bias_ref, rows_ref, table_ref):
    lane = lanes_of((544, 128))
    sub = lax.broadcasted_iota(jnp.int32, (544, 128), 0)
    rows_ref[...] = jnp.zeros_like(rows_ref)
    for a in range(17):
        rows_ref[a : a + 1, 0:17] = bias_ref[a, pl.ds(head, 1), :]
    spread = jnp.concatenate(
        [jnp.broadcast_to(rows_ref[a : a + 1, :], (32, 128)) for a in range(17)], axis=0
    )
    b_index = sub & 31
    column = jnp.sum(jnp.where(lane == b_index, spread, 0.0), axis=1, keepdims=True)
    skewed = jnp.where(b_index < 17, column * LOG2E, MASKED)
    query_col = lane & 15
    for bit in (1, 2, 4, 8):
        skewed = jnp.where((query_col & bit) > 0, pltpu.roll(skewed, bit, 0), skewed)
    blocks = skewed.reshape(17, 32, 128)
    empty = jnp.full((7, 32, 128), MASKED, jnp.float32)
    padded = jnp.concatenate([empty, blocks, empty], axis=0)
    query_row = lanes_of((24, 32, 128)) >> 4
    table = padded[7:31]
    for row in range(1, 8):
        table = jnp.where(query_row == row, padded[7 - row : 31 - row], table)
    table = table.reshape(3, 8, 4, 8, 128)
    for chunk in range(4):
        table_ref[:, chunk] = table[:, :, chunk]


def contract_bias(sums_ref, skew_ref, bias_out_ref):
    query_row = lanes_of((17, 8, 128)) >> 4
    for chunk in range(4):
        by_row = sums_ref[:, chunk].reshape(24, 8, 128)
        picked = by_row[0:17]
        for row in range(1, 8):
            picked = jnp.where(query_row == row, by_row[row : row + 17], picked)
        skew_ref[:, chunk] = picked
    skewed = skew_ref[...].reshape(544, 128)
    query_col = lanes_of((544, 128)) & 15
    for bit in (1, 2, 4, 8):
        skewed = jnp.where((query_col & bit) > 0, pltpu.roll(skewed, 544 - bit, 0), skewed)
    skewed = jnp.concatenate([skewed, jnp.zeros((96, 128), jnp.float32)], axis=0)
    total = lax.dot_general(
        jnp.ones((8, 128), jnp.float32),
        skewed,
        (((1,), (1,)), ((), ())),
        precision=lax.Precision.HIGHEST,
        preferred_element_type=jnp.float32,
    )
    bias_out_ref[...] = jnp.broadcast_to(total[0:1, :][None], bias_out_ref.shape)


def main_kernel(
    occ_ref,
    bias_ref,
    x_ref,
    inner_ref,
    outer_ref,
    dq_ref,
    own_ref,
    out_inner_ref,
    out_outer_ref,
    bias_out_ref,
    rows_ref,
    table_ref,
    sums_ref,
    skew_ref,
    kv_ref,
    kt_ref,
    qg_ref,
    p_ref,
):
    head = lax.axis_index("row")
    col = lax.axis_index("col")
    col_count = occ_ref.shape[1]
    even = (col & 1) == 0
    build_table(head, bias_ref, rows_ref, table_ref)
    low = lanes_of((128, 128)) < 64
    sums_ref[...] = jnp.zeros_like(sums_ref)

    def filled(row, at):
        inside = (at >= 0) & (at < col_count)
        return inside & (occ_ref[row, jnp.clip(at, 0, col_count - 1)] > 0)

    def penalty(row, at):
        return jnp.where(filled(row, at), jnp.float32(0.0), jnp.float32(MASKED))

    marks = []
    for j in range(8):
        inner, outer = inner_ref[j], outer_ref[j]
        kv_ref[256 * j : 256 * j + 64] = jnp.where(even, outer, inner)
        kv_ref[256 * j + 64 : 256 * j + 192] = x_ref[j, 128:256]
        kv_ref[256 * j + 192 : 256 * j + 256] = jnp.where(even, inner, outer)
        flipped = jnp.transpose(kv_ref[256 * j : 256 * j + 256])
        kt_ref[:, 256 * j : 256 * j + 256] = flipped[0:64]
        query_grad = x_ref[j, 0:128]
        zero = jnp.zeros_like(query_grad)
        qg_ref[256 * j : 256 * j + 128] = jnp.where(low, query_grad, zero)
        qg_ref[256 * j + 128 : 256 * j + 256] = jnp.where(low, zero, query_grad)
        own = penalty(j, col)
        marks.append((penalty(j, col - 1), own, own, penalty(j, col + 1)))

    def window(i):
        steps = [step for step in range(3) if 0 <= i - 1 + step < 8]
        return steps, i - 1 + steps[0], len(steps)

    def products(i):
        _, first, count = window(i)
        return lax.dot_general(
            kv_ref[256 * first : 256 * (first + count)],
            qg_ref[256 * i : 256 * i + 256],
            (((1,), (1,)), ((), ())),
            preferred_element_type=jnp.float32,
        )

    def softmax(i, both):
        steps, first, count = window(i)
        scores, grads = both[:, 0:128], both[:, 128:256]
        shifted = []
        for step in steps:
            for chunk in range(4):
                at = 256 * (step - steps[0]) + 64 * chunk
                bias = table_ref[step, chunk].reshape(64, 128) + marks[i - 1 + step][chunk]
                shifted.append(scores[at : at + 64] * LOG2E + bias)
        shifted = jnp.concatenate(shifted, axis=0)
        top = jnp.max(shifted, axis=0, keepdims=True)
        exponent = jnp.exp2(shifted - top)
        total = jnp.sum(exponent, axis=0, keepdims=True)
        weighted = jnp.sum(exponent * grads, axis=0, keepdims=True)
        inverse = 1.0 / total
        delta = weighted * inverse
        used = jnp.where(filled(i, col), jnp.float32(1.0), jnp.float32(0.0))
        weights = exponent * (inverse * used)
        grad_scores = weights * (grads - delta)
        sums_ref[steps[0] : steps[-1] + 1] += grad_scores.reshape(count, 4, 8, 8, 128)
        return weights.astype(jnp.bfloat16), grad_scores.astype(jnp.bfloat16)

    def gradients(i, weights_low, grad_low):
        steps, first, count = window(i)
        shares = jnp.dot(
            jnp.concatenate([grad_low, weights_low], axis=1),
            qg_ref[256 * i : 256 * i + 256],
            preferred_element_type=jnp.float32,
        )
        grad_query = jnp.dot(
            kt_ref[:, 256 * first : 256 * (first + count)],
            grad_low,
            preferred_element_type=jnp.float32,
        )
        dq_ref[i] = (grad_query * 0.125).astype(jnp.bfloat16)
        for step in steps:
            at = 256 * (step - steps[0])
            j = i - 1 + step
            part = shares[at : at + 256]
            if not (step == 2 or i == 0):
                part = part + p_ref[j]
            if step == 0 or i == 7:
                left, right = part[0:64], part[192:256]
                out_inner_ref[j] = jnp.where(even, right, left).astype(jnp.bfloat16)
                own_ref[j] = part[64:192]
                out_outer_ref[j] = jnp.where(even, left, right).astype(jnp.bfloat16)
            else:
                p_ref[j] = part

    both = {i: products(i) for i in range(8)}
    pairs = [softmax(i, both[i]) for i in range(8)]
    for i in range(8):
        gradients(i, *pairs[i])
    contract_bias(sums_ref, skew_ref, bias_out_ref)


def main(occupied, bias, blocks, inner, outer, col_count):
    halo = jax.ShapeDtypeStruct((8, 64, 128), jnp.bfloat16)
    return pl.pallas_call(
        main_kernel,
        out_shape=(
            halo,
            jax.ShapeDtypeStruct((8, 128, 128), jnp.float32),
            halo,
            halo,
            jax.ShapeDtypeStruct((col_count, 1, 640), jnp.float32),
        ),
        in_specs=[SMEM_SPEC] + [VMEM_SPEC] * 4,
        out_specs=(VMEM_SPEC,) * 5,
        scratch_shapes=[
            pltpu.VMEM((24, 128), jnp.float32),
            pltpu.VMEM((3, 4, 8, 8, 128), jnp.float32),
            pltpu.VMEM((3, 4, 8, 8, 128), jnp.float32),
            pltpu.VMEM((17, 4, 8, 128), jnp.float32),
            pltpu.VMEM((2048, 128), jnp.bfloat16),
            pltpu.VMEM((64, 2048), jnp.bfloat16),
            pltpu.VMEM((2048, 128), jnp.bfloat16),
            pltpu.VMEM((8, 256, 128), jnp.float32),
        ],
        compiler_params=pltpu.CompilerParams(vmem_limit_bytes=24 << 20),
        name="attention_backward",
    )(occupied, bias, blocks, inner, outer)


def combine_kernel(dq_ref, own_ref, inner_ref, outer_ref, bias_ref, out_ref):
    even = (lax.axis_index("col") & 1) == 0
    summed = jnp.sum(bias_ref[...], axis=0)
    rows = [summed[:, 128 * k : 128 * k + 128] for k in range(5)]
    total = jnp.concatenate(rows + [jnp.zeros((3, 128), jnp.float32)], axis=0)
    high = total.astype(jnp.bfloat16).astype(jnp.float32)
    rest = total - high
    middle = rest.astype(jnp.bfloat16).astype(jnp.float32)
    pieces = jnp.concatenate([high, middle, rest - middle, jnp.zeros_like(total)], axis=0)
    pieces = pieces.astype(jnp.bfloat16)
    for i in range(8):
        out_ref[i, 0:64] = dq_ref[i]
        inner, outer = inner_ref[i].astype(jnp.float32), outer_ref[i].astype(jnp.float32)
        for at, share in (
            (0, jnp.where(even, outer, inner)),
            (64, jnp.where(even, inner, outer)),
        ):
            summed = own_ref[i, at : at + 64] + share
            out_ref[i, 64 + at : 128 + at] = summed.astype(jnp.bfloat16)
        out_ref[i, 192:224] = pieces


def combine(dq, own, inner, outer, bias):
    return pl.pallas_call(
        combine_kernel,
        out_shape=jax.ShapeDtypeStruct((8, 224, 128), jnp.bfloat16),
        in_specs=[VMEM_SPEC] * 5,
        out_specs=VMEM_SPEC,
        compiler_params=pltpu.CompilerParams(vmem_limit_bytes=8 << 20),
        name="combine",
    )(dq, own, inner, outer, bias)


def unpack_kernel(z_ref, gq_hbm, gk_hbm, gv_hbm, gb_ref, gq_ref, gk_ref, gv_ref, bias_ref, sems):
    low = lanes_of((128, 128)) < 64
    copies = [
        pltpu.make_async_copy(source, target, sems.at[at])
        for at, (source, target) in enumerate(
            ((gq_ref, gq_hbm), (gk_ref, gk_hbm), (gv_ref, gv_hbm))
        )
    ]

    def load(head, first, last):
        return z_ref[head, first:last].astype(jnp.float32)

    def by_rows(block):
        split = block.reshape(2, 8, 8, 128)
        return jnp.concatenate([split[0], split[1]], axis=1)

    for pair in range(4):
        lanes = pl.ds(128 * pair, 128)
        both = jnp.concatenate([load(2 * pair, 0, 64), load(2 * pair + 1, 0, 64)], axis=0)
        gq_ref[:, :, lanes] = jnp.transpose(both).reshape(8, 16, 128).astype(jnp.bfloat16)
    copies[0].start()
    for pair in range(4):
        lanes = pl.ds(128 * pair, 128)
        key = jnp.where(
            low, load(2 * pair, 64, 192), swap_halves(load(2 * pair + 1, 64, 192))
        )
        gk_ref[:, :, lanes] = by_rows(key).astype(jnp.bfloat16)
    copies[1].start()
    for pair in range(4):
        lanes = pl.ds(128 * pair, 128)
        value = jnp.where(
            low, swap_halves(load(2 * pair, 64, 192)), load(2 * pair + 1, 64, 192)
        )
        gv_ref[:, :, lanes] = by_rows(value).astype(jnp.bfloat16)
    copies[2].start()
    for head in range(8):
        pieces = load(head, 192, 224)
        bias_ref[head] = pieces[0:8] + pieces[8:16] + pieces[16:24]
    for a in range(17):
        row = bias_ref[:, a // 4, :]
        if a % 4:
            row = pltpu.roll(row, 128 - 32 * (a % 4), 1)
        gb_ref[a] = row[:, 0:17]
    for copy in copies:
        copy.wait()


def unpack(blocks):
    token = jax.ShapeDtypeStruct((8, 16, 512), jnp.bfloat16)
    return pl.pallas_call(
        unpack_kernel,
        out_shape=(token, token, token, jax.ShapeDtypeStruct((17, 8, 17), jnp.float32)),
        in_specs=[VMEM_SPEC],
        out_specs=(HBM_SPEC,) * 3 + (VMEM_SPEC,),
        scratch_shapes=[pltpu.VMEM((8, 16, 512), jnp.bfloat16)] * 3
        + [pltpu.VMEM((8, 8, 128), jnp.float32), pltpu.SemaphoreType.DMA((3,))],
        compiler_params=pltpu.CompilerParams(vmem_limit_bytes=8 << 20),
        name="unpack",
    )(blocks)


def shards(queries, keys, values, grad_out, rel_bias, occupied):
    col_count = lax.axis_size("col")
    within = [(i, i ^ 1) for i in range(col_count)]
    between = [(i, i - 1 if i % 2 == 0 else i + 1) for i in range(1, col_count - 1)]
    odd = lax.axis_index("col") & 1
    packed = pack(queries, keys, values, grad_out)
    blocks = lax.all_to_all(packed, "row", 0, 0)
    inner = lax.ppermute(
        lax.dynamic_slice_in_dim(blocks, 192 - 64 * odd, 64, axis=1), "col", within
    )
    outer = lax.ppermute(
        lax.dynamic_slice_in_dim(blocks, 128 + 64 * odd, 64, axis=1), "col", between
    )
    bias = jnp.transpose(rel_bias, (1, 0, 2))
    dq, own, out_inner, out_outer, bias_part = main(
        occupied, bias, blocks, inner, outer, col_count
    )
    inner_share = lax.ppermute(out_inner, "col", within)
    outer_share = lax.ppermute(out_outer, "col", between)
    bias_parts = lax.all_to_all(bias_part, "col", 0, 0)
    returned = lax.all_to_all(combine(dq, own, inner_share, outer_share, bias_parts), "row", 0, 0)
    grad_query, grad_key, grad_value, grad_bias = unpack(returned)
    return grad_query, grad_key, grad_value, jnp.transpose(grad_bias, (1, 0, 2))


def solution(mesh):
    token = P("row", "col", None)
    return jax.shard_map(
        shards,
        mesh=mesh,
        in_specs=(token, token, token, token, P(), P()),
        out_specs=(token, token, token, P()),
        check_vma=False,
    )
```

```python
import functools

import jax
import jax.numpy as jnp
from jax import lax
from jax.experimental import pallas as pl
from jax.experimental.pallas import tpu as pltpu
from jax.sharding import PartitionSpec as P

LOG2E = 1.4426950408889634
MASKED = -1e30
VMEM_SPEC = pl.BlockSpec(memory_space=pltpu.VMEM)
HBM_SPEC = pl.BlockSpec(memory_space=pltpu.HBM)


def lanes_of(shape):
    return lax.broadcasted_iota(jnp.int32, shape, len(shape) - 1)


def swap_halves(array):
    return pltpu.roll(array, 64, 1)


def pack_kernel(
    q_hbm, k_hbm, v_hbm, g_hbm, out_hbm, q_ref, k_ref, v_ref, g_ref, out_ref, in_sems, out_sems
):
    copies = [
        pltpu.make_async_copy(source, target, in_sems.at[at])
        for at, (source, target) in enumerate(
            ((q_hbm, q_ref), (g_hbm, g_ref), (k_hbm, k_ref), (v_hbm, v_ref))
        )
    ]
    for copy in copies:
        copy.start()
    low = lanes_of((128, 128)) < 64

    def load(ref, pair):
        return ref[:, :, 128 * pair : 128 * pair + 128].astype(jnp.float32)

    def by_halves(block):
        split = block.reshape(8, 2, 8, 128)
        return jnp.concatenate([split[:, half].reshape(64, 128) for half in range(2)], axis=0)

    def store(pair, at, first, second):
        even = jnp.where(low, first, swap_halves(second))
        odd = jnp.where(low, swap_halves(first), second)
        out_ref[2 * pair, at : at + 128, :] = even.astype(jnp.bfloat16)
        out_ref[2 * pair + 1, at : at + 128, :] = odd.astype(jnp.bfloat16)

    copies[0].wait()
    copies[1].wait()
    for pair in range(4):
        query = load(q_ref, pair).reshape(128, 128) * 0.125
        store(pair, 0, query, load(g_ref, pair).reshape(128, 128))
    copies[2].wait()
    copies[3].wait()
    returns = []
    for pair in range(4):
        store(pair, 128, by_halves(load(k_ref, pair)), by_halves(load(v_ref, pair)))
        heads = pl.ds(2 * pair, 2)
        returns.append(
            pltpu.make_async_copy(out_ref.at[heads], out_hbm.at[heads], out_sems.at[pair])
        )
        returns[-1].start()
    for copy in returns:
        copy.wait()


def pack(queries, keys, values, grad_out):
    return pl.pallas_call(
        pack_kernel,
        out_shape=jax.ShapeDtypeStruct((8, 256, 128), jnp.bfloat16),
        in_specs=[HBM_SPEC] * 4,
        out_specs=HBM_SPEC,
        scratch_shapes=[pltpu.VMEM((8, 16, 512), jnp.bfloat16)] * 4
        + [
            pltpu.VMEM((8, 256, 128), jnp.bfloat16),
            pltpu.SemaphoreType.DMA((4,)),
            pltpu.SemaphoreType.DMA((4,)),
        ],
        compiler_params=pltpu.CompilerParams(vmem_limit_bytes=60 << 20),
        name="pack",
    )(queries, keys, values, grad_out)


def build_table(head, bias_ref, rows_ref, table_ref):
    lane = lanes_of((544, 128))
    sub = lax.broadcasted_iota(jnp.int32, (544, 128), 0)
    rows_ref[...] = jnp.zeros_like(rows_ref)
    for a in range(17):
        rows_ref[a : a + 1, 0:17] = bias_ref[a, pl.ds(head, 1), :]
    spread = jnp.concatenate(
        [jnp.broadcast_to(rows_ref[a : a + 1, :], (32, 128)) for a in range(17)], axis=0
    )
    b_index = sub & 31
    column = jnp.sum(jnp.where(lane == b_index, spread, 0.0), axis=1, keepdims=True)
    skewed = jnp.where(b_index < 17, column * LOG2E, MASKED)
    query_col = lane & 15
    for bit in (1, 2, 4, 8):
        skewed = jnp.where((query_col & bit) > 0, pltpu.roll(skewed, bit, 0), skewed)
    blocks = skewed.reshape(17, 32, 128)
    empty = jnp.full((7, 32, 128), MASKED, jnp.float32)
    padded = jnp.concatenate([empty, blocks, empty], axis=0)
    query_row = lanes_of((24, 32, 128)) >> 4
    table = padded[7:31]
    for row in range(1, 8):
        table = jnp.where(query_row == row, padded[7 - row : 31 - row], table)
    table = table.reshape(3, 8, 4, 8, 128)
    for chunk in range(4):
        table_ref[:, chunk] = table[:, :, chunk]


def contract_bias(sums_ref, skew_ref, bias_out_ref):
    query_row = lanes_of((17, 8, 128)) >> 4
    for chunk in range(4):
        by_row = sums_ref[:, chunk].reshape(24, 8, 128)
        picked = by_row[0:17]
        for row in range(1, 8):
            picked = jnp.where(query_row == row, by_row[row : row + 17], picked)
        skew_ref[:, chunk] = picked
    skewed = skew_ref[...].reshape(544, 128)
    query_col = lanes_of((544, 128)) & 15
    for bit in (1, 2, 4, 8):
        skewed = jnp.where((query_col & bit) > 0, pltpu.roll(skewed, 544 - bit, 0), skewed)
    skewed = jnp.concatenate([skewed, jnp.zeros((96, 128), jnp.float32)], axis=0)
    total = lax.dot_general(
        jnp.ones((8, 128), jnp.float32),
        skewed,
        (((1,), (1,)), ((), ())),
        precision=lax.Precision.HIGHEST,
        preferred_element_type=jnp.float32,
    )
    bias_out_ref[...] = jnp.broadcast_to(total[0:1, :][None], bias_out_ref.shape)


def main_kernel(
    occ_ref,
    bias_ref,
    x_ref,
    inner_ref,
    outer_ref,
    dq_ref,
    own_ref,
    out_inner_ref,
    out_outer_ref,
    bias_out_ref,
    rows_ref,
    table_ref,
    sums_ref,
    skew_ref,
    kv_ref,
    kt_ref,
    qg_ref,
    p_ref,
):
    head = lax.axis_index("row")
    col = lax.axis_index("col")
    even = (col & 1) == 0
    build_table(head, bias_ref, rows_ref, table_ref)
    low = lanes_of((128, 128)) < 64
    sums_ref[...] = jnp.zeros_like(sums_ref)

    lane = lanes_of(occ_ref.shape)

    def filled(at):
        column = jnp.sum(jnp.where(lane == at, occ_ref[...], 0), axis=1, keepdims=True)
        return jnp.broadcast_to(column, (8, 128)) > 0

    own_filled = filled(col)
    used = jnp.where(own_filled, 1.0, 0.0)
    own_mark = jnp.where(own_filled, 0.0, MASKED)
    left_mark = jnp.where(filled(col - 1), 0.0, MASKED)
    right_mark = jnp.where(filled(col + 1), 0.0, MASKED)
    chunk_marks = (left_mark, own_mark, own_mark, right_mark)

    for j in range(8):
        inner, outer = inner_ref[j], outer_ref[j]
        kv_ref[256 * j : 256 * j + 64] = jnp.where(even, outer, inner)
        kv_ref[256 * j + 64 : 256 * j + 192] = x_ref[j, 128:256]
        kv_ref[256 * j + 192 : 256 * j + 256] = jnp.where(even, inner, outer)
        flipped = jnp.transpose(kv_ref[256 * j : 256 * j + 256])
        kt_ref[:, 256 * j : 256 * j + 256] = flipped[0:64]
        query_grad = x_ref[j, 0:128]
        zero = jnp.zeros_like(query_grad)
        qg_ref[256 * j : 256 * j + 128] = jnp.where(low, query_grad, zero)
        qg_ref[256 * j + 128 : 256 * j + 256] = jnp.where(low, zero, query_grad)

    def window(i):
        steps = [step for step in range(3) if 0 <= i - 1 + step < 8]
        return steps, i - 1 + steps[0], len(steps)

    def products(i):
        _, first, count = window(i)
        return lax.dot_general(
            kv_ref[256 * first : 256 * (first + count)],
            qg_ref[256 * i : 256 * i + 256],
            (((1,), (1,)), ((), ())),
            preferred_element_type=jnp.float32,
        )

    def softmax(i, both):
        steps, first, count = window(i)
        scores, grads = both[:, 0:128], both[:, 128:256]
        shifted = []
        for step in steps:
            for chunk in range(4):
                at = 256 * (step - steps[0]) + 64 * chunk
                row = i - 1 + step
                mark = chunk_marks[chunk][row : row + 1]
                bias = table_ref[step, chunk].reshape(64, 128) + mark
                shifted.append(scores[at : at + 64] * LOG2E + bias)
        shifted = jnp.concatenate(shifted, axis=0)
        top = jnp.max(shifted, axis=0, keepdims=True)
        exponent = jnp.exp2(shifted - top)
        total = jnp.sum(exponent, axis=0, keepdims=True)
        weighted = jnp.sum(exponent * grads, axis=0, keepdims=True)
        inverse = 1.0 / total
        delta = weighted * inverse
        weights = exponent * (inverse * used[i : i + 1])
        grad_scores = weights * (grads - delta)
        sums_ref[steps[0] : steps[-1] + 1] += grad_scores.reshape(count, 4, 8, 8, 128)
        return weights.astype(jnp.bfloat16), grad_scores.astype(jnp.bfloat16)

    def gradients(i, weights_low, grad_low):
        steps, first, count = window(i)
        shares = jnp.dot(
            jnp.concatenate([grad_low, weights_low], axis=1),
            qg_ref[256 * i : 256 * i + 256],
            preferred_element_type=jnp.float32,
        )
        grad_query = jnp.dot(
            kt_ref[:, 256 * first : 256 * (first + count)],
            grad_low,
            preferred_element_type=jnp.float32,
        )
        dq_ref[i] = (grad_query * 0.125).astype(jnp.bfloat16)
        for step in steps:
            at = 256 * (step - steps[0])
            j = i - 1 + step
            part = shares[at : at + 256]
            if not (step == 2 or i == 0):
                part = part + p_ref[j]
            if step == 0 or i == 7:
                left, right = part[0:64], part[192:256]
                out_inner_ref[j] = jnp.where(even, right, left).astype(jnp.bfloat16)
                own_ref[j] = part[64:192]
                out_outer_ref[j] = jnp.where(even, left, right).astype(jnp.bfloat16)
            else:
                p_ref[j] = part

    both = {i: products(i) for i in range(8)}
    pairs = [softmax(i, both[i]) for i in range(8)]
    for i in range(8):
        gradients(i, *pairs[i])
    contract_bias(sums_ref, skew_ref, bias_out_ref)


def main(occupied, bias, blocks, inner, outer, col_count):
    halo = jax.ShapeDtypeStruct((8, 64, 128), jnp.bfloat16)
    return pl.pallas_call(
        main_kernel,
        out_shape=(
            halo,
            jax.ShapeDtypeStruct((8, 128, 128), jnp.float32),
            halo,
            halo,
            jax.ShapeDtypeStruct((col_count, 1, 640), jnp.float32),
        ),
        in_specs=[VMEM_SPEC] * 5,
        out_specs=(VMEM_SPEC,) * 5,
        scratch_shapes=[
            pltpu.VMEM((24, 128), jnp.float32),
            pltpu.VMEM((3, 4, 8, 8, 128), jnp.float32),
            pltpu.VMEM((3, 4, 8, 8, 128), jnp.float32),
            pltpu.VMEM((17, 4, 8, 128), jnp.float32),
            pltpu.VMEM((2048, 128), jnp.bfloat16),
            pltpu.VMEM((64, 2048), jnp.bfloat16),
            pltpu.VMEM((2048, 128), jnp.bfloat16),
            pltpu.VMEM((8, 256, 128), jnp.float32),
        ],
        compiler_params=pltpu.CompilerParams(vmem_limit_bytes=24 << 20),
        name="attention_backward",
    )(occupied, bias, blocks, inner, outer)


def combine_kernel(dq_ref, own_ref, inner_ref, outer_ref, bias_ref, out_ref):
    even = (lax.axis_index("col") & 1) == 0
    summed = jnp.sum(bias_ref[...], axis=0)
    high = summed.astype(jnp.bfloat16).astype(jnp.float32)
    rest = summed - high
    middle = rest.astype(jnp.bfloat16).astype(jnp.float32)
    rows = [
        piece[:, 128 * k : 128 * k + 128]
        for piece in (high, middle, rest - middle)
        for k in range(5)
    ]
    rows.append(jnp.zeros((1, 128), jnp.float32))
    pieces = jnp.concatenate(rows, axis=0).astype(jnp.bfloat16)
    for i in range(8):
        out_ref[i, 0:64] = dq_ref[i]
        inner, outer = inner_ref[i].astype(jnp.float32), outer_ref[i].astype(jnp.float32)
        for at, share in (
            (0, jnp.where(even, outer, inner)),
            (64, jnp.where(even, inner, outer)),
        ):
            summed = own_ref[i, at : at + 64] + share
            out_ref[i, 64 + at : 128 + at] = summed.astype(jnp.bfloat16)
        out_ref[i, 192:208] = pieces


def combine(dq, own, inner, outer, bias):
    return pl.pallas_call(
        combine_kernel,
        out_shape=jax.ShapeDtypeStruct((8, 208, 128), jnp.bfloat16),
        in_specs=[VMEM_SPEC] * 5,
        out_specs=VMEM_SPEC,
        compiler_params=pltpu.CompilerParams(vmem_limit_bytes=8 << 20),
        name="combine",
    )(dq, own, inner, outer, bias)


def unpack_kernel(z_ref, gq_hbm, gk_hbm, gv_hbm, gb_ref, gq_ref, gk_ref, gv_ref, pieces_ref, sems):
    low = lanes_of((128, 128)) < 64
    copies = [
        pltpu.make_async_copy(source, target, sems.at[at])
        for at, (source, target) in enumerate(
            ((gq_ref, gq_hbm), (gk_ref, gk_hbm), (gv_ref, gv_hbm))
        )
    ]

    def load(head, first, last):
        return z_ref[head, first:last].astype(jnp.float32)

    def by_rows(block):
        split = block.reshape(2, 8, 8, 128)
        return jnp.concatenate([split[0], split[1]], axis=1)

    for pair in range(4):
        lanes = pl.ds(128 * pair, 128)
        both = jnp.concatenate([load(2 * pair, 0, 64), load(2 * pair + 1, 0, 64)], axis=0)
        gq_ref[:, :, lanes] = jnp.transpose(both).reshape(8, 16, 128).astype(jnp.bfloat16)
    copies[0].start()
    for pair in range(4):
        lanes = pl.ds(128 * pair, 128)
        key = jnp.where(
            low, load(2 * pair, 64, 192), swap_halves(load(2 * pair + 1, 64, 192))
        )
        gk_ref[:, :, lanes] = by_rows(key).astype(jnp.bfloat16)
    copies[1].start()
    for pair in range(4):
        lanes = pl.ds(128 * pair, 128)
        value = jnp.where(
            low, swap_halves(load(2 * pair, 64, 192)), load(2 * pair + 1, 64, 192)
        )
        gv_ref[:, :, lanes] = by_rows(value).astype(jnp.bfloat16)
    copies[2].start()
    for head in range(8):
        pieces_ref[head] = load(head, 192, 208)
    for a in range(17):
        k = a // 4
        row = pieces_ref[:, k, :] + pieces_ref[:, k + 5, :] + pieces_ref[:, k + 10, :]
        if a % 4:
            row = pltpu.roll(row, 128 - 32 * (a % 4), 1)
        gb_ref[a] = row[:, 0:17]
    for copy in copies:
        copy.wait()


def unpack(blocks):
    token = jax.ShapeDtypeStruct((8, 16, 512), jnp.bfloat16)
    return pl.pallas_call(
        unpack_kernel,
        out_shape=(token, token, token, jax.ShapeDtypeStruct((17, 8, 17), jnp.float32)),
        in_specs=[VMEM_SPEC],
        out_specs=(HBM_SPEC,) * 3 + (VMEM_SPEC,),
        scratch_shapes=[pltpu.VMEM((8, 16, 512), jnp.bfloat16)] * 3
        + [pltpu.VMEM((8, 16, 128), jnp.float32), pltpu.SemaphoreType.DMA((3,))],
        compiler_params=pltpu.CompilerParams(vmem_limit_bytes=8 << 20),
        name="unpack",
    )(blocks)


def shards(queries, keys, values, grad_out, rel_bias, occupied):
    col_count = lax.axis_size("col")
    within = [(i, i ^ 1) for i in range(col_count)]
    between = [(i, i - 1 if i % 2 == 0 else i + 1) for i in range(1, col_count - 1)]
    odd = lax.axis_index("col") & 1
    packed = pack(queries, keys, values, grad_out)
    blocks = lax.all_to_all(packed, "row", 0, 0)
    inner = lax.ppermute(
        lax.dynamic_slice_in_dim(blocks, 192 - 64 * odd, 64, axis=1), "col", within
    )
    outer = lax.ppermute(
        lax.dynamic_slice_in_dim(blocks, 128 + 64 * odd, 64, axis=1), "col", between
    )
    bias = jnp.transpose(rel_bias, (1, 0, 2))
    dq, own, out_inner, out_outer, bias_part = main(
        occupied, bias, blocks, inner, outer, col_count
    )
    outer_share = lax.ppermute(out_outer, "col", between)
    inner_share = lax.ppermute(out_inner, "col", within)
    bias_parts = lax.all_to_all(bias_part, "col", 0, 0)
    returned = lax.all_to_all(combine(dq, own, inner_share, outer_share, bias_parts), "row", 0, 0)
    grad_query, grad_key, grad_value, grad_bias = unpack(returned)
    return grad_query, grad_key, grad_value, jnp.transpose(grad_bias, (1, 0, 2))


def solution(mesh):
    token = P("row", "col", None)
    return jax.shard_map(
        shards,
        mesh=mesh,
        in_specs=(token, token, token, token, P(), P()),
        out_specs=(token, token, token, P()),
        check_vma=False,
    )
```

```python
import functools

import jax
import jax.numpy as jnp
from jax import lax
from jax.experimental import pallas as pl
from jax.experimental.pallas import tpu as pltpu
from jax.sharding import PartitionSpec as P

LOG2E = 1.4426950408889634
MASKED = -1e30
VMEM_SPEC = pl.BlockSpec(memory_space=pltpu.VMEM)
HBM_SPEC = pl.BlockSpec(memory_space=pltpu.HBM)


def lanes_of(shape):
    return lax.broadcasted_iota(jnp.int32, shape, len(shape) - 1)


def swap_halves(array):
    return pltpu.roll(array, 64, 1)


def even_col():
    return (lax.axis_index("col") & 1) == 0


def pack_kernel(q_hbm, k_hbm, v_hbm, g_hbm, out_ref, q_ref, k_ref, v_ref, g_ref, sems):
    copies = [
        pltpu.make_async_copy(source, target, sems.at[at])
        for at, (source, target) in enumerate(
            ((q_hbm, q_ref), (g_hbm, g_ref), (k_hbm, k_ref), (v_hbm, v_ref))
        )
    ]
    for copy in copies:
        copy.start()
    low = lanes_of((128, 128)) < 64
    even_col_here = even_col()

    def load(ref, pair):
        return ref[:, :, 128 * pair : 128 * pair + 128].astype(jnp.float32)

    def by_halves(block):
        split = block.reshape(8, 2, 8, 128)
        left, right = split[:, 0].reshape(64, 128), split[:, 1].reshape(64, 128)
        inner = jnp.where(even_col_here, right, left)
        outer = jnp.where(even_col_here, left, right)
        return jnp.concatenate([inner, outer], axis=0)

    def store(pair, at, first, second):
        even = jnp.where(low, first, swap_halves(second))
        odd = jnp.where(low, swap_halves(first), second)
        out_ref[2 * pair, at : at + 128, :] = even.astype(jnp.bfloat16)
        out_ref[2 * pair + 1, at : at + 128, :] = odd.astype(jnp.bfloat16)

    copies[0].wait()
    copies[1].wait()
    for pair in range(4):
        query = load(q_ref, pair).reshape(128, 128) * 0.125
        store(pair, 0, query, load(g_ref, pair).reshape(128, 128))
    copies[2].wait()
    copies[3].wait()
    for pair in range(4):
        store(pair, 128, by_halves(load(k_ref, pair)), by_halves(load(v_ref, pair)))


def pack(queries, keys, values, grad_out):
    return pl.pallas_call(
        pack_kernel,
        out_shape=jax.ShapeDtypeStruct((8, 256, 128), jnp.bfloat16),
        in_specs=[HBM_SPEC] * 4,
        out_specs=VMEM_SPEC,
        scratch_shapes=[pltpu.VMEM((8, 16, 512), jnp.bfloat16)] * 4
        + [pltpu.SemaphoreType.DMA((4,))],
        compiler_params=pltpu.CompilerParams(vmem_limit_bytes=8 << 20),
        name="pack",
    )(
        *(
            pltpu.with_memory_space_constraint(array, pltpu.HBM)
            for array in (queries, keys, values, grad_out)
        )
    )


def chunk_place(chunk):
    return jnp.where(even_col(), 3 - chunk, chunk)


def build_table(head, bias_ref, rows_ref, table_ref):
    lane = lanes_of((544, 128))
    sub = lax.broadcasted_iota(jnp.int32, (544, 128), 0)
    rows_ref[...] = jnp.zeros_like(rows_ref)
    for a in range(17):
        rows_ref[a : a + 1, 0:17] = bias_ref[a, pl.ds(head, 1), :]
    spread = jnp.concatenate(
        [jnp.broadcast_to(rows_ref[a : a + 1, :], (32, 128)) for a in range(17)], axis=0
    )
    b_index = sub & 31
    column = jnp.sum(jnp.where(lane == b_index, spread, 0.0), axis=1, keepdims=True)
    skewed = jnp.where(b_index < 17, column * LOG2E, MASKED)
    query_col = lane & 15
    for bit in (1, 2, 4, 8):
        skewed = jnp.where((query_col & bit) > 0, pltpu.roll(skewed, bit, 0), skewed)
    blocks = skewed.reshape(17, 32, 128)
    empty = jnp.full((7, 32, 128), MASKED, jnp.float32)
    padded = jnp.concatenate([empty, blocks, empty], axis=0)
    query_row = lanes_of((24, 32, 128)) >> 4
    table = padded[7:31]
    for row in range(1, 8):
        table = jnp.where(query_row == row, padded[7 - row : 31 - row], table)
    table = table.reshape(3, 8, 4, 8, 128)
    for chunk in range(4):
        table_ref[:, chunk_place(chunk)] = table[:, :, chunk]


def contract_bias(sums_ref, skew_ref, bias_out_ref):
    query_row = lanes_of((17, 8, 128)) >> 4
    for chunk in range(4):
        by_row = sums_ref[:, chunk_place(chunk)].reshape(24, 8, 128)
        picked = by_row[0:17]
        for row in range(1, 8):
            picked = jnp.where(query_row == row, by_row[row : row + 17], picked)
        skew_ref[:, chunk] = picked
    skewed = skew_ref[...].reshape(544, 128)
    query_col = lanes_of((544, 128)) & 15
    for bit in (1, 2, 4, 8):
        skewed = jnp.where((query_col & bit) > 0, pltpu.roll(skewed, 544 - bit, 0), skewed)
    skewed = jnp.concatenate([skewed, jnp.zeros((96, 128), jnp.float32)], axis=0)
    total = lax.dot_general(
        jnp.ones((8, 128), jnp.float32),
        skewed,
        (((1,), (1,)), ((), ())),
        precision=lax.Precision.HIGHEST,
        preferred_element_type=jnp.float32,
    )
    bias_out_ref[...] = jnp.broadcast_to(total[0:1, :][None], bias_out_ref.shape)


def main_kernel(
    occ_ref,
    bias_ref,
    x_ref,
    inner_ref,
    outer_ref,
    dq_ref,
    own_ref,
    out_inner_ref,
    out_outer_ref,
    bias_out_ref,
    rows_ref,
    table_ref,
    sums_ref,
    skew_ref,
    kv_ref,
    kt_ref,
    qg_ref,
    p_ref,
):
    head = lax.axis_index("row")
    col = lax.axis_index("col")
    even = even_col()
    build_table(head, bias_ref, rows_ref, table_ref)
    low = lanes_of((128, 128)) < 64
    sums_ref[...] = jnp.zeros_like(sums_ref)

    lane = lanes_of(occ_ref.shape)

    def filled(at):
        column = jnp.sum(jnp.where(lane == at, occ_ref[...], 0), axis=1, keepdims=True)
        return jnp.broadcast_to(column, (8, 128)) > 0

    own_filled = filled(col)
    used = jnp.where(own_filled, 1.0, 0.0)
    own_mark = jnp.where(own_filled, 0.0, MASKED)
    inner_mark = jnp.where(filled(jnp.where(even, col + 1, col - 1)), 0.0, MASKED)
    outer_mark = jnp.where(filled(jnp.where(even, col - 1, col + 1)), 0.0, MASKED)
    chunk_marks = (inner_mark, own_mark, own_mark, outer_mark)

    for j in range(8):
        kv_ref[256 * j : 256 * j + 64] = inner_ref[j]
        kv_ref[256 * j + 64 : 256 * j + 192] = x_ref[j, 128:256]
        kv_ref[256 * j + 192 : 256 * j + 256] = outer_ref[j]
        flipped = jnp.transpose(kv_ref[256 * j : 256 * j + 256])
        kt_ref[:, 256 * j : 256 * j + 256] = flipped[0:64]
        query_grad = x_ref[j, 0:128]
        zero = jnp.zeros_like(query_grad)
        qg_ref[256 * j : 256 * j + 128] = jnp.where(low, query_grad, zero)
        qg_ref[256 * j + 128 : 256 * j + 256] = jnp.where(low, zero, query_grad)

    def window(i):
        steps = [step for step in range(3) if 0 <= i - 1 + step < 8]
        return steps, i - 1 + steps[0], len(steps)

    def products(i):
        _, first, count = window(i)
        return lax.dot_general(
            kv_ref[256 * first : 256 * (first + count)],
            qg_ref[256 * i : 256 * i + 256],
            (((1,), (1,)), ((), ())),
            preferred_element_type=jnp.float32,
        )

    def softmax(i, both):
        steps, first, count = window(i)
        scores, grads = both[:, 0:128], both[:, 128:256]
        shifted = []
        for step in steps:
            for chunk in range(4):
                at = 256 * (step - steps[0]) + 64 * chunk
                row = i - 1 + step
                mark = chunk_marks[chunk][row : row + 1]
                bias = table_ref[step, chunk].reshape(64, 128) + mark
                shifted.append(scores[at : at + 64] * LOG2E + bias)
        shifted = jnp.concatenate(shifted, axis=0)
        top = jnp.max(shifted, axis=0, keepdims=True)
        exponent = jnp.exp2(shifted - top)
        total = jnp.sum(exponent, axis=0, keepdims=True)
        weighted = jnp.sum(exponent * grads, axis=0, keepdims=True)
        inverse = 1.0 / total
        delta = weighted * inverse
        weights = exponent * (inverse * used[i : i + 1])
        grad_scores = weights * (grads - delta)
        sums_ref[steps[0] : steps[-1] + 1] += grad_scores.reshape(count, 4, 8, 8, 128)
        return weights.astype(jnp.bfloat16), grad_scores.astype(jnp.bfloat16)

    def gradients(i, weights_low, grad_low):
        steps, first, count = window(i)
        shares = jnp.dot(
            jnp.concatenate([grad_low, weights_low], axis=1),
            qg_ref[256 * i : 256 * i + 256],
            preferred_element_type=jnp.float32,
        )
        grad_query = jnp.dot(
            kt_ref[:, 256 * first : 256 * (first + count)],
            grad_low,
            preferred_element_type=jnp.float32,
        )
        dq_ref[i] = (grad_query * 0.125).astype(jnp.bfloat16)
        for step in steps:
            at = 256 * (step - steps[0])
            j = i - 1 + step
            part = shares[at : at + 256]
            if not (step == 2 or i == 0):
                part = part + p_ref[j]
            if step == 0 or i == 7:
                out_inner_ref[j] = part[0:64].astype(jnp.bfloat16)
                own_ref[j] = part[64:192]
                out_outer_ref[j] = part[192:256].astype(jnp.bfloat16)
            else:
                p_ref[j] = part

    both = {i: products(i) for i in range(8)}
    pairs = [softmax(i, both[i]) for i in range(8)]
    for i in range(8):
        gradients(i, *pairs[i])
    contract_bias(sums_ref, skew_ref, bias_out_ref)


def main(occupied, bias, blocks, inner, outer, col_count):
    halo = jax.ShapeDtypeStruct((8, 64, 128), jnp.bfloat16)
    return pl.pallas_call(
        main_kernel,
        out_shape=(
            halo,
            jax.ShapeDtypeStruct((8, 128, 128), jnp.float32),
            halo,
            halo,
            jax.ShapeDtypeStruct((col_count, 1, 640), jnp.float32),
        ),
        in_specs=[VMEM_SPEC] * 5,
        out_specs=(VMEM_SPEC,) * 5,
        scratch_shapes=[
            pltpu.VMEM((24, 128), jnp.float32),
            pltpu.VMEM((3, 4, 8, 8, 128), jnp.float32),
            pltpu.VMEM((3, 4, 8, 8, 128), jnp.float32),
            pltpu.VMEM((17, 4, 8, 128), jnp.float32),
            pltpu.VMEM((2048, 128), jnp.bfloat16),
            pltpu.VMEM((64, 2048), jnp.bfloat16),
            pltpu.VMEM((2048, 128), jnp.bfloat16),
            pltpu.VMEM((8, 256, 128), jnp.float32),
        ],
        compiler_params=pltpu.CompilerParams(vmem_limit_bytes=24 << 20),
        name="attention_backward",
    )(occupied, bias, blocks, inner, outer)


def combine_kernel(dq_ref, own_ref, inner_ref, outer_ref, bias_ref, out_ref):
    summed = jnp.sum(bias_ref[...], axis=0)
    high = summed.astype(jnp.bfloat16).astype(jnp.float32)
    rest = summed - high
    middle = rest.astype(jnp.bfloat16).astype(jnp.float32)
    rows = [
        piece[:, 128 * k : 128 * k + 128]
        for piece in (high, middle, rest - middle)
        for k in range(5)
    ]
    rows.append(jnp.zeros((1, 128), jnp.float32))
    pieces = jnp.concatenate(rows, axis=0).astype(jnp.bfloat16)
    for i in range(8):
        out_ref[i, 0:64] = dq_ref[i]
        for at, ref in ((0, inner_ref), (64, outer_ref)):
            summed = own_ref[i, at : at + 64] + ref[i].astype(jnp.float32)
            out_ref[i, 64 + at : 128 + at] = summed.astype(jnp.bfloat16)
        out_ref[i, 192:208] = pieces


def combine(dq, own, inner, outer, bias):
    return pl.pallas_call(
        combine_kernel,
        out_shape=jax.ShapeDtypeStruct((8, 208, 128), jnp.bfloat16),
        in_specs=[VMEM_SPEC] * 5,
        out_specs=VMEM_SPEC,
        compiler_params=pltpu.CompilerParams(vmem_limit_bytes=8 << 20),
        name="combine",
    )(dq, own, inner, outer, bias)


def unpack_kernel(z_ref, gq_hbm, gk_hbm, gv_hbm, gb_ref, gq_ref, gk_ref, gv_ref, pieces_ref, sems):
    even_col_here = even_col()
    low = lanes_of((128, 128)) < 64
    copies = [
        pltpu.make_async_copy(source, target, sems.at[at])
        for at, (source, target) in enumerate(
            ((gq_ref, gq_hbm), (gk_ref, gk_hbm), (gv_ref, gv_hbm))
        )
    ]

    def load(head, first, last):
        return z_ref[head, first:last].astype(jnp.float32)

    def by_rows(block):
        inner, outer = block[0:64].reshape(8, 8, 128), block[64:128].reshape(8, 8, 128)
        left = jnp.where(even_col_here, outer, inner)
        right = jnp.where(even_col_here, inner, outer)
        return jnp.concatenate([left, right], axis=1)

    for pair in range(4):
        lanes = pl.ds(128 * pair, 128)
        both = jnp.concatenate([load(2 * pair, 0, 64), load(2 * pair + 1, 0, 64)], axis=0)
        gq_ref[:, :, lanes] = jnp.transpose(both).reshape(8, 16, 128).astype(jnp.bfloat16)
    copies[0].start()
    for pair in range(4):
        lanes = pl.ds(128 * pair, 128)
        key = jnp.where(
            low, load(2 * pair, 64, 192), swap_halves(load(2 * pair + 1, 64, 192))
        )
        gk_ref[:, :, lanes] = by_rows(key).astype(jnp.bfloat16)
    copies[1].start()
    for pair in range(4):
        lanes = pl.ds(128 * pair, 128)
        value = jnp.where(
            low, swap_halves(load(2 * pair, 64, 192)), load(2 * pair + 1, 64, 192)
        )
        gv_ref[:, :, lanes] = by_rows(value).astype(jnp.bfloat16)
    copies[2].start()
    for head in range(8):
        pieces_ref[head] = load(head, 192, 208)
    for a in range(17):
        k = a // 4
        row = pieces_ref[:, k, :] + pieces_ref[:, k + 5, :] + pieces_ref[:, k + 10, :]
        if a % 4:
            row = pltpu.roll(row, 128 - 32 * (a % 4), 1)
        gb_ref[a] = row[:, 0:17]
    for copy in copies:
        copy.wait()


def unpack(blocks):
    token = jax.ShapeDtypeStruct((8, 16, 512), jnp.bfloat16)
    return pl.pallas_call(
        unpack_kernel,
        out_shape=(token, token, token, jax.ShapeDtypeStruct((17, 8, 17), jnp.float32)),
        in_specs=[VMEM_SPEC],
        out_specs=(HBM_SPEC,) * 3 + (VMEM_SPEC,),
        scratch_shapes=[pltpu.VMEM((8, 16, 512), jnp.bfloat16)] * 3
        + [pltpu.VMEM((8, 16, 128), jnp.float32), pltpu.SemaphoreType.DMA((3,))],
        compiler_params=pltpu.CompilerParams(vmem_limit_bytes=8 << 20),
        name="unpack",
    )(blocks)


def shards(queries, keys, values, grad_out, rel_bias, occupied):
    col_count = lax.axis_size("col")
    within = [(i, i ^ 1) for i in range(col_count)]
    between = [(i, i - 1 if i % 2 == 0 else i + 1) for i in range(1, col_count - 1)]
    packed = pack(queries, keys, values, grad_out)
    blocks = lax.all_to_all(packed, "row", 0, 0)
    inner = lax.ppermute(blocks[:, 128:192], "col", within)
    outer = lax.ppermute(blocks[:, 192:256], "col", between)
    bias = jnp.transpose(rel_bias, (1, 0, 2))
    dq, own, out_inner, out_outer, bias_part = main(
        occupied, bias, blocks, inner, outer, col_count
    )
    outer_share = lax.ppermute(out_outer, "col", between)
    inner_share = lax.ppermute(out_inner, "col", within)
    bias_parts = lax.all_to_all(bias_part, "col", 0, 0)
    returned = lax.all_to_all(combine(dq, own, inner_share, outer_share, bias_parts), "row", 0, 0)
    grad_query, grad_key, grad_value, grad_bias = unpack(returned)
    return grad_query, grad_key, grad_value, jnp.transpose(grad_bias, (1, 0, 2))


def solution(mesh):
    token = P("row", "col", None)
    return jax.shard_map(
        shards,
        mesh=mesh,
        in_specs=(token, token, token, token, P(), P()),
        out_specs=(token, token, token, P()),
        check_vma=False,
    )
```

```python
import functools

import jax
import jax.numpy as jnp
from jax import lax
from jax.experimental import pallas as pl
from jax.experimental.pallas import tpu as pltpu
from jax.sharding import PartitionSpec as P

LOG2E = 1.4426950408889634
MASKED = -1e30
VMEM_SPEC = pl.BlockSpec(memory_space=pltpu.VMEM)
HBM_SPEC = pl.BlockSpec(memory_space=pltpu.HBM)


def lanes_of(shape):
    return lax.broadcasted_iota(jnp.int32, shape, len(shape) - 1)


def swap_halves(array):
    return pltpu.roll(array, 64, 1)


def even_col():
    return (lax.axis_index("col") & 1) == 0


def pack_kernel(q_hbm, k_hbm, v_hbm, g_hbm, out_ref, q_ref, k_ref, v_ref, g_ref, sems):
    copies = [
        pltpu.make_async_copy(source, target, sems.at[at])
        for at, (source, target) in enumerate(
            ((q_hbm, q_ref), (g_hbm, g_ref), (k_hbm, k_ref), (v_hbm, v_ref))
        )
    ]
    for copy in copies:
        copy.start()
    low = lanes_of((128, 128)) < 64
    even_col_here = even_col()

    def load(ref, pair):
        return ref[:, :, 128 * pair : 128 * pair + 128].astype(jnp.float32)

    def by_halves(block):
        split = block.reshape(8, 2, 8, 128)
        left, right = split[:, 0].reshape(64, 128), split[:, 1].reshape(64, 128)
        inner = jnp.where(even_col_here, right, left)
        outer = jnp.where(even_col_here, left, right)
        return jnp.concatenate([inner, outer], axis=0)

    def store(pair, at, first, second):
        even = jnp.where(low, first, swap_halves(second))
        odd = jnp.where(low, swap_halves(first), second)
        out_ref[2 * pair, at : at + 128, :] = even.astype(jnp.bfloat16)
        out_ref[2 * pair + 1, at : at + 128, :] = odd.astype(jnp.bfloat16)

    copies[0].wait()
    copies[1].wait()
    for pair in range(4):
        query = load(q_ref, pair).reshape(128, 128) * 0.125
        store(pair, 0, query, load(g_ref, pair).reshape(128, 128))
    copies[2].wait()
    copies[3].wait()
    for pair in range(4):
        store(pair, 128, by_halves(load(k_ref, pair)), by_halves(load(v_ref, pair)))


def pack(queries, keys, values, grad_out):
    return pl.pallas_call(
        pack_kernel,
        out_shape=jax.ShapeDtypeStruct((8, 256, 128), jnp.bfloat16),
        in_specs=[HBM_SPEC] * 4,
        out_specs=VMEM_SPEC,
        scratch_shapes=[pltpu.VMEM((8, 16, 512), jnp.bfloat16)] * 4
        + [pltpu.SemaphoreType.DMA((4,))],
        compiler_params=pltpu.CompilerParams(vmem_limit_bytes=8 << 20),
        name="pack",
    )(
        *(
            pltpu.with_memory_space_constraint(array, pltpu.HBM)
            for array in (queries, keys, values, grad_out)
        )
    )


def chunk_place(chunk):
    return jnp.where(even_col(), 3 - chunk, chunk)


def build_table(head, bias_ref, rows_ref, table_ref):
    lane = lanes_of((544, 128))
    sub = lax.broadcasted_iota(jnp.int32, (544, 128), 0)
    rows_ref[...] = jnp.zeros_like(rows_ref)
    for a in range(17):
        rows_ref[a : a + 1, 0:17] = bias_ref[a, pl.ds(head, 1), :]
    spread = jnp.concatenate(
        [jnp.broadcast_to(rows_ref[a : a + 1, :], (32, 128)) for a in range(17)], axis=0
    )
    b_index = sub & 31
    column = jnp.sum(jnp.where(lane == b_index, spread, 0.0), axis=1, keepdims=True)
    skewed = jnp.where(b_index < 17, column * LOG2E, MASKED)
    query_col = lane & 15
    for bit in (1, 2, 4, 8):
        skewed = jnp.where((query_col & bit) > 0, pltpu.roll(skewed, bit, 0), skewed)
    blocks = skewed.reshape(17, 32, 128)
    empty = jnp.full((7, 32, 128), MASKED, jnp.float32)
    padded = jnp.concatenate([empty, blocks, empty], axis=0)
    query_row = lanes_of((24, 32, 128)) >> 4
    table = padded[7:31]
    for row in range(1, 8):
        table = jnp.where(query_row == row, padded[7 - row : 31 - row], table)
    table = table.reshape(3, 8, 4, 8, 128)
    for chunk in range(4):
        table_ref[:, chunk_place(chunk)] = table[:, :, chunk]


def contract_bias(sums_ref, skew_ref, bias_out_ref):
    query_row = lanes_of((17, 8, 128)) >> 4
    for chunk in range(4):
        by_row = sums_ref[:, chunk_place(chunk)].reshape(24, 8, 128)
        picked = by_row[0:17]
        for row in range(1, 8):
            picked = jnp.where(query_row == row, by_row[row : row + 17], picked)
        skew_ref[:, chunk] = picked
    skewed = skew_ref[...].reshape(544, 128)
    query_col = lanes_of((544, 128)) & 15
    for bit in (1, 2, 4, 8):
        skewed = jnp.where((query_col & bit) > 0, pltpu.roll(skewed, 544 - bit, 0), skewed)
    skewed = jnp.concatenate([skewed, jnp.zeros((96, 128), jnp.float32)], axis=0)
    total = lax.dot_general(
        jnp.ones((8, 128), jnp.float32),
        skewed,
        (((1,), (1,)), ((), ())),
        precision=lax.Precision.HIGHEST,
        preferred_element_type=jnp.float32,
    )
    bias_out_ref[...] = jnp.broadcast_to(total[0:1, :][None], bias_out_ref.shape)


def window(i):
    steps = [step for step in range(3) if 0 <= i - 1 + step < 8]
    return steps, i - 1 + steps[0], len(steps)


def against(keys, queries):
    return lax.dot_general(
        keys, queries, (((1,), (1,)), ((), ())), preferred_element_type=jnp.float32
    )


def own_kernel(bias_ref, x_ref, table_ref, qg_ref, scores_ref, rows_ref):
    low = lanes_of((128, 128)) < 64
    for j in range(8):
        query_grad = x_ref[j, 0:128]
        zero = jnp.zeros_like(query_grad)
        qg_ref[256 * j : 256 * j + 128] = jnp.where(low, query_grad, zero)
        qg_ref[256 * j + 128 : 256 * j + 256] = jnp.where(low, zero, query_grad)
    for i in range(8):
        steps, first, count = window(i)
        keys = x_ref[first : first + count, 128:256].reshape(128 * count, 128)
        at = 128 * steps[0]
        scores_ref[i, at : at + 128 * count] = against(keys, qg_ref[256 * i : 256 * i + 256])
    build_table(lax.axis_index("row"), bias_ref, rows_ref, table_ref)


def own_scores(bias, blocks):
    return pl.pallas_call(
        own_kernel,
        out_shape=(
            jax.ShapeDtypeStruct((3, 4, 8, 8, 128), jnp.float32),
            jax.ShapeDtypeStruct((2048, 128), jnp.bfloat16),
            jax.ShapeDtypeStruct((8, 384, 256), jnp.float32),
        ),
        in_specs=[VMEM_SPEC] * 2,
        out_specs=(VMEM_SPEC,) * 3,
        scratch_shapes=[pltpu.VMEM((24, 128), jnp.float32)],
        compiler_params=pltpu.CompilerParams(vmem_limit_bytes=8 << 20),
        name="own_scores",
    )(bias, blocks)


def main_kernel(
    occ_ref,
    table_ref,
    qg_ref,
    scores_ref,
    x_ref,
    inner_ref,
    outer_ref,
    dq_ref,
    own_ref,
    out_inner_ref,
    out_outer_ref,
    bias_out_ref,
    sums_ref,
    skew_ref,
    kv_ref,
    kt_ref,
    p_ref,
):
    col = lax.axis_index("col")
    even = even_col()
    sums_ref[...] = jnp.zeros_like(sums_ref)

    lane = lanes_of(occ_ref.shape)

    def filled(at):
        column = jnp.sum(jnp.where(lane == at, occ_ref[...], 0), axis=1, keepdims=True)
        return jnp.broadcast_to(column, (8, 128)) > 0

    own_filled = filled(col)
    used = jnp.where(own_filled, 1.0, 0.0)
    own_mark = jnp.where(own_filled, 0.0, MASKED)
    inner_mark = jnp.where(filled(jnp.where(even, col + 1, col - 1)), 0.0, MASKED)
    outer_mark = jnp.where(filled(jnp.where(even, col - 1, col + 1)), 0.0, MASKED)
    chunk_marks = (inner_mark, own_mark, own_mark, outer_mark)

    for j in range(8):
        kv_ref[256 * j : 256 * j + 64] = inner_ref[j]
        kv_ref[256 * j + 64 : 256 * j + 192] = x_ref[j, 128:256]
        kv_ref[256 * j + 192 : 256 * j + 256] = outer_ref[j]
        flipped = jnp.transpose(kv_ref[256 * j : 256 * j + 256])
        kt_ref[:, 256 * j : 256 * j + 256] = flipped[0:64]

    def products(i):
        _, first, count = window(i)
        return [
            against(
                ref[first : first + count].reshape(64 * count, 128),
                qg_ref[256 * i : 256 * i + 256],
            )
            for ref in (inner_ref, outer_ref)
        ]

    def softmax(i, both):
        steps, first, count = window(i)
        shifted, grads = [], []
        for step in steps:
            halo = 64 * (step - steps[0])
            parts = (
                both[0][halo : halo + 64],
                scores_ref[i, 128 * step : 128 * step + 64],
                scores_ref[i, 128 * step + 64 : 128 * step + 128],
                both[1][halo : halo + 64],
            )
            for chunk in range(4):
                row = i - 1 + step
                mark = chunk_marks[chunk][row : row + 1]
                bias = table_ref[step, chunk].reshape(64, 128) + mark
                shifted.append(parts[chunk][:, 0:128] * LOG2E + bias)
                grads.append(parts[chunk][:, 128:256])
        shifted, grads = jnp.concatenate(shifted, axis=0), jnp.concatenate(grads, axis=0)
        top = jnp.max(shifted, axis=0, keepdims=True)
        exponent = jnp.exp2(shifted - top)
        total = jnp.sum(exponent, axis=0, keepdims=True)
        weighted = jnp.sum(exponent * grads, axis=0, keepdims=True)
        inverse = 1.0 / total
        delta = weighted * inverse
        weights = exponent * (inverse * used[i : i + 1])
        grad_scores = weights * (grads - delta)
        sums_ref[steps[0] : steps[-1] + 1] += grad_scores.reshape(count, 4, 8, 8, 128)
        return weights.astype(jnp.bfloat16), grad_scores.astype(jnp.bfloat16)

    def gradients(i, weights_low, grad_low):
        steps, first, count = window(i)
        shares = jnp.dot(
            jnp.concatenate([grad_low, weights_low], axis=1),
            qg_ref[256 * i : 256 * i + 256],
            preferred_element_type=jnp.float32,
        )
        grad_query = jnp.dot(
            kt_ref[:, 256 * first : 256 * (first + count)],
            grad_low,
            preferred_element_type=jnp.float32,
        )
        dq_ref[i] = (grad_query * 0.125).astype(jnp.bfloat16)
        for step in steps:
            at = 256 * (step - steps[0])
            j = i - 1 + step
            part = shares[at : at + 256]
            if not (step == 2 or i == 0):
                part = part + p_ref[j]
            if step == 0 or i == 7:
                out_inner_ref[j] = part[0:64].astype(jnp.bfloat16)
                own_ref[j] = part[64:192]
                out_outer_ref[j] = part[192:256].astype(jnp.bfloat16)
            else:
                p_ref[j] = part

    both = {i: products(i) for i in range(8)}
    pairs = [softmax(i, both[i]) for i in range(8)]
    for i in range(8):
        gradients(i, *pairs[i])
    contract_bias(sums_ref, skew_ref, bias_out_ref)


def main(occupied, table, qg, scores, blocks, inner, outer, col_count):
    halo = jax.ShapeDtypeStruct((8, 64, 128), jnp.bfloat16)
    return pl.pallas_call(
        main_kernel,
        out_shape=(
            halo,
            jax.ShapeDtypeStruct((8, 128, 128), jnp.float32),
            halo,
            halo,
            jax.ShapeDtypeStruct((col_count, 1, 640), jnp.float32),
        ),
        in_specs=[VMEM_SPEC] * 7,
        out_specs=(VMEM_SPEC,) * 5,
        scratch_shapes=[
            pltpu.VMEM((3, 4, 8, 8, 128), jnp.float32),
            pltpu.VMEM((17, 4, 8, 128), jnp.float32),
            pltpu.VMEM((2048, 128), jnp.bfloat16),
            pltpu.VMEM((64, 2048), jnp.bfloat16),
            pltpu.VMEM((8, 256, 128), jnp.float32),
        ],
        compiler_params=pltpu.CompilerParams(vmem_limit_bytes=24 << 20),
        name="attention_backward",
    )(occupied, table, qg, scores, blocks, inner, outer)


def combine_kernel(dq_ref, own_ref, inner_ref, outer_ref, bias_ref, out_ref):
    summed = jnp.sum(bias_ref[...], axis=0)
    high = summed.astype(jnp.bfloat16).astype(jnp.float32)
    rest = summed - high
    middle = rest.astype(jnp.bfloat16).astype(jnp.float32)
    rows = [
        piece[:, 128 * k : 128 * k + 128]
        for piece in (high, middle, rest - middle)
        for k in range(5)
    ]
    rows.append(jnp.zeros((1, 128), jnp.float32))
    pieces = jnp.concatenate(rows, axis=0).astype(jnp.bfloat16)
    for i in range(8):
        out_ref[i, 0:64] = dq_ref[i]
        for at, ref in ((0, inner_ref), (64, outer_ref)):
            summed = own_ref[i, at : at + 64] + ref[i].astype(jnp.float32)
            out_ref[i, 64 + at : 128 + at] = summed.astype(jnp.bfloat16)
        out_ref[i, 192:208] = pieces


def combine(dq, own, inner, outer, bias):
    return pl.pallas_call(
        combine_kernel,
        out_shape=jax.ShapeDtypeStruct((8, 208, 128), jnp.bfloat16),
        in_specs=[VMEM_SPEC] * 5,
        out_specs=VMEM_SPEC,
        compiler_params=pltpu.CompilerParams(vmem_limit_bytes=8 << 20),
        name="combine",
    )(dq, own, inner, outer, bias)


def unpack_kernel(z_ref, gq_hbm, gk_hbm, gv_hbm, gb_ref, gq_ref, gk_ref, gv_ref, pieces_ref, sems):
    even_col_here = even_col()
    low = lanes_of((128, 128)) < 64
    copies = [
        pltpu.make_async_copy(source, target, sems.at[at])
        for at, (source, target) in enumerate(
            ((gq_ref, gq_hbm), (gk_ref, gk_hbm), (gv_ref, gv_hbm))
        )
    ]

    def load(head, first, last):
        return z_ref[head, first:last].astype(jnp.float32)

    def by_rows(block):
        inner, outer = block[0:64].reshape(8, 8, 128), block[64:128].reshape(8, 8, 128)
        left = jnp.where(even_col_here, outer, inner)
        right = jnp.where(even_col_here, inner, outer)
        return jnp.concatenate([left, right], axis=1)

    for pair in range(4):
        lanes = pl.ds(128 * pair, 128)
        both = jnp.concatenate([load(2 * pair, 0, 64), load(2 * pair + 1, 0, 64)], axis=0)
        gq_ref[:, :, lanes] = jnp.transpose(both).reshape(8, 16, 128).astype(jnp.bfloat16)
    copies[0].start()
    for pair in range(4):
        lanes = pl.ds(128 * pair, 128)
        key = jnp.where(
            low, load(2 * pair, 64, 192), swap_halves(load(2 * pair + 1, 64, 192))
        )
        gk_ref[:, :, lanes] = by_rows(key).astype(jnp.bfloat16)
    copies[1].start()
    for pair in range(4):
        lanes = pl.ds(128 * pair, 128)
        value = jnp.where(
            low, swap_halves(load(2 * pair, 64, 192)), load(2 * pair + 1, 64, 192)
        )
        gv_ref[:, :, lanes] = by_rows(value).astype(jnp.bfloat16)
    copies[2].start()
    for head in range(8):
        pieces_ref[head] = load(head, 192, 208)
    for a in range(17):
        k = a // 4
        row = pieces_ref[:, k, :] + pieces_ref[:, k + 5, :] + pieces_ref[:, k + 10, :]
        if a % 4:
            row = pltpu.roll(row, 128 - 32 * (a % 4), 1)
        gb_ref[a] = row[:, 0:17]
    for copy in copies:
        copy.wait()


def unpack(blocks):
    token = jax.ShapeDtypeStruct((8, 16, 512), jnp.bfloat16)
    return pl.pallas_call(
        unpack_kernel,
        out_shape=(token, token, token, jax.ShapeDtypeStruct((17, 8, 17), jnp.float32)),
        in_specs=[VMEM_SPEC],
        out_specs=(HBM_SPEC,) * 3 + (VMEM_SPEC,),
        scratch_shapes=[pltpu.VMEM((8, 16, 512), jnp.bfloat16)] * 3
        + [pltpu.VMEM((8, 16, 128), jnp.float32), pltpu.SemaphoreType.DMA((3,))],
        compiler_params=pltpu.CompilerParams(vmem_limit_bytes=8 << 20),
        name="unpack",
    )(blocks)


def shards(queries, keys, values, grad_out, rel_bias, occupied):
    col_count = lax.axis_size("col")
    within = [(i, i ^ 1) for i in range(col_count)]
    between = [(i, i - 1 if i % 2 == 0 else i + 1) for i in range(1, col_count - 1)]
    packed = pack(queries, keys, values, grad_out)
    blocks = lax.all_to_all(packed, "row", 0, 0)
    inner = lax.ppermute(blocks[:, 128:192], "col", within)
    outer = lax.ppermute(blocks[:, 192:256], "col", between)
    bias = jnp.transpose(rel_bias, (1, 0, 2))
    dq, own, out_inner, out_outer, bias_part = main(
        occupied, *own_scores(bias, blocks), blocks, inner, outer, col_count
    )
    outer_share = lax.ppermute(out_outer, "col", between)
    inner_share = lax.ppermute(out_inner, "col", within)
    bias_parts = lax.all_to_all(bias_part, "col", 0, 0)
    returned = lax.all_to_all(combine(dq, own, inner_share, outer_share, bias_parts), "row", 0, 0)
    grad_query, grad_key, grad_value, grad_bias = unpack(returned)
    return grad_query, grad_key, grad_value, jnp.transpose(grad_bias, (1, 0, 2))


def solution(mesh):
    token = P("row", "col", None)
    return jax.shard_map(
        shards,
        mesh=mesh,
        in_specs=(token, token, token, token, P(), P()),
        out_specs=(token, token, token, P()),
        check_vma=False,
    )
```

```python
import functools

import jax
import jax.numpy as jnp
from jax import lax
from jax.experimental import pallas as pl
from jax.experimental.pallas import tpu as pltpu
from jax.sharding import PartitionSpec as P

LOG2E = 1.4426950408889634
MASKED = -1e30
VMEM_SPEC = pl.BlockSpec(memory_space=pltpu.VMEM)
HBM_SPEC = pl.BlockSpec(memory_space=pltpu.HBM)


def lanes_of(shape):
    return lax.broadcasted_iota(jnp.int32, shape, len(shape) - 1)


def swap_halves(array):
    return pltpu.roll(array, 64, 1)


def even_col():
    return (lax.axis_index("col") & 1) == 0


def pack_kernel(q_hbm, k_hbm, v_hbm, g_hbm, out_ref, q_ref, k_ref, v_ref, g_ref, sems):
    copies = [
        pltpu.make_async_copy(source, target, sems.at[at])
        for at, (source, target) in enumerate(
            ((q_hbm, q_ref), (g_hbm, g_ref), (k_hbm, k_ref), (v_hbm, v_ref))
        )
    ]
    for copy in copies:
        copy.start()
    low = lanes_of((128, 128)) < 64
    even_col_here = even_col()

    def load(ref, pair):
        return ref[:, :, 128 * pair : 128 * pair + 128].astype(jnp.float32)

    def by_halves(block):
        split = block.reshape(8, 2, 8, 128)
        left, right = split[:, 0].reshape(64, 128), split[:, 1].reshape(64, 128)
        inner = jnp.where(even_col_here, right, left)
        outer = jnp.where(even_col_here, left, right)
        return jnp.concatenate([inner, outer], axis=0)

    def store(pair, at, first, second):
        even = jnp.where(low, first, swap_halves(second))
        odd = jnp.where(low, swap_halves(first), second)
        out_ref[2 * pair, at : at + 128, :] = even.astype(jnp.bfloat16)
        out_ref[2 * pair + 1, at : at + 128, :] = odd.astype(jnp.bfloat16)

    copies[0].wait()
    copies[1].wait()
    for pair in range(4):
        query = load(q_ref, pair).reshape(128, 128) * 0.125
        store(pair, 0, query, load(g_ref, pair).reshape(128, 128))
    copies[2].wait()
    copies[3].wait()
    for pair in range(4):
        store(pair, 128, by_halves(load(k_ref, pair)), by_halves(load(v_ref, pair)))


def pack(queries, keys, values, grad_out):
    return pl.pallas_call(
        pack_kernel,
        out_shape=jax.ShapeDtypeStruct((8, 256, 128), jnp.bfloat16),
        in_specs=[HBM_SPEC] * 4,
        out_specs=VMEM_SPEC,
        scratch_shapes=[pltpu.VMEM((8, 16, 512), jnp.bfloat16)] * 4
        + [pltpu.SemaphoreType.DMA((4,))],
        compiler_params=pltpu.CompilerParams(vmem_limit_bytes=8 << 20),
        name="pack",
    )(
        *(
            pltpu.with_memory_space_constraint(array, pltpu.HBM)
            for array in (queries, keys, values, grad_out)
        )
    )


def chunk_place(chunk):
    return jnp.where(even_col(), 3 - chunk, chunk)


def build_table(head, bias_ref, rows_ref, table_ref):
    lane = lanes_of((544, 128))
    sub = lax.broadcasted_iota(jnp.int32, (544, 128), 0)
    rows_ref[...] = jnp.zeros_like(rows_ref)
    for a in range(17):
        rows_ref[a : a + 1, 0:17] = bias_ref[a, pl.ds(head, 1), :]
    spread = jnp.concatenate(
        [jnp.broadcast_to(rows_ref[a : a + 1, :], (32, 128)) for a in range(17)], axis=0
    )
    b_index = sub & 31
    column = jnp.sum(jnp.where(lane == b_index, spread, 0.0), axis=1, keepdims=True)
    skewed = jnp.where(b_index < 17, column * LOG2E, MASKED)
    query_col = lane & 15
    for bit in (1, 2, 4, 8):
        skewed = jnp.where((query_col & bit) > 0, pltpu.roll(skewed, bit, 0), skewed)
    blocks = skewed.reshape(17, 32, 128)
    empty = jnp.full((7, 32, 128), MASKED, jnp.float32)
    padded = jnp.concatenate([empty, blocks, empty], axis=0)
    query_row = lanes_of((24, 32, 128)) >> 4
    table = padded[7:31]
    for row in range(1, 8):
        table = jnp.where(query_row == row, padded[7 - row : 31 - row], table)
    table = table.reshape(3, 8, 4, 8, 128)
    for chunk in range(4):
        table_ref[:, chunk_place(chunk)] = table[:, :, chunk]


def contract_bias(sums_ref, skew_ref, bias_out_ref):
    query_row = lanes_of((17, 8, 128)) >> 4
    for chunk in range(4):
        by_row = sums_ref[:, chunk_place(chunk)].reshape(24, 8, 128)
        picked = by_row[0:17]
        for row in range(1, 8):
            picked = jnp.where(query_row == row, by_row[row : row + 17], picked)
        skew_ref[:, chunk] = picked
    skewed = skew_ref[...].reshape(544, 128)
    query_col = lanes_of((544, 128)) & 15
    for bit in (1, 2, 4, 8):
        skewed = jnp.where((query_col & bit) > 0, pltpu.roll(skewed, 544 - bit, 0), skewed)
    skewed = jnp.concatenate([skewed, jnp.zeros((96, 128), jnp.float32)], axis=0)
    total = lax.dot_general(
        jnp.ones((8, 128), jnp.float32),
        skewed,
        (((1,), (1,)), ((), ())),
        precision=lax.Precision.HIGHEST,
        preferred_element_type=jnp.float32,
    )
    bias_out_ref[...] = jnp.broadcast_to(total[0:1, :][None], bias_out_ref.shape)


def window(i):
    steps = [step for step in range(3) if 0 <= i - 1 + step < 8]
    return steps, i - 1 + steps[0], len(steps)


def against(keys, queries):
    return lax.dot_general(
        keys, queries, (((1,), (1,)), ((), ())), preferred_element_type=jnp.float32
    )


def own_kernel(bias_ref, x_ref, table_ref, qg_ref, scores_ref, rows_ref):
    low = lanes_of((128, 128)) < 64
    for j in range(8):
        query_grad = x_ref[j, 0:128]
        zero = jnp.zeros_like(query_grad)
        qg_ref[256 * j : 256 * j + 128] = jnp.where(low, query_grad, zero)
        qg_ref[256 * j + 128 : 256 * j + 256] = jnp.where(low, zero, query_grad)
    for i in range(8):
        steps, first, count = window(i)
        keys = x_ref[first : first + count, 128:256].reshape(128 * count, 128)
        at = 128 * steps[0]
        scores_ref[i, at : at + 128 * count] = against(keys, qg_ref[256 * i : 256 * i + 256])
    build_table(lax.axis_index("row"), bias_ref, rows_ref, table_ref)


def own_scores(bias, blocks):
    return pl.pallas_call(
        own_kernel,
        out_shape=(
            jax.ShapeDtypeStruct((3, 4, 8, 8, 128), jnp.float32),
            jax.ShapeDtypeStruct((2048, 128), jnp.bfloat16),
            jax.ShapeDtypeStruct((8, 384, 256), jnp.float32),
        ),
        in_specs=[VMEM_SPEC] * 2,
        out_specs=(VMEM_SPEC,) * 3,
        scratch_shapes=[pltpu.VMEM((24, 128), jnp.float32)],
        compiler_params=pltpu.CompilerParams(vmem_limit_bytes=8 << 20),
        name="own_scores",
    )(bias, blocks)


def main_kernel(
    occ_ref,
    table_ref,
    qg_ref,
    scores_ref,
    x_ref,
    inner_ref,
    outer_ref,
    low_ref,
    kt_ref,
    own_ref,
    out_inner_ref,
    out_outer_ref,
    bias_out_ref,
    sums_ref,
    skew_ref,
    kv_ref,
    p_ref,
):
    col = lax.axis_index("col")
    even = even_col()
    sums_ref[...] = jnp.zeros_like(sums_ref)

    lane = lanes_of(occ_ref.shape)

    def filled(at):
        column = jnp.sum(jnp.where(lane == at, occ_ref[...], 0), axis=1, keepdims=True)
        return jnp.broadcast_to(column, (8, 128)) > 0

    own_filled = filled(col)
    used = jnp.where(own_filled, 1.0, 0.0)
    own_mark = jnp.where(own_filled, 0.0, MASKED)
    inner_mark = jnp.where(filled(jnp.where(even, col + 1, col - 1)), 0.0, MASKED)
    outer_mark = jnp.where(filled(jnp.where(even, col - 1, col + 1)), 0.0, MASKED)
    chunk_marks = (inner_mark, own_mark, own_mark, outer_mark)

    for j in range(8):
        kv_ref[256 * j : 256 * j + 64] = inner_ref[j]
        kv_ref[256 * j + 64 : 256 * j + 192] = x_ref[j, 128:256]
        kv_ref[256 * j + 192 : 256 * j + 256] = outer_ref[j]
        flipped = jnp.transpose(kv_ref[256 * j : 256 * j + 256])
        kt_ref[:, 256 * j : 256 * j + 256] = flipped[0:64]

    def products(i):
        _, first, count = window(i)
        return [
            against(
                ref[first : first + count].reshape(64 * count, 128),
                qg_ref[256 * i : 256 * i + 256],
            )
            for ref in (inner_ref, outer_ref)
        ]

    def softmax(i, both):
        steps, first, count = window(i)
        shifted, grads = [], []
        for step in steps:
            halo = 64 * (step - steps[0])
            parts = (
                both[0][halo : halo + 64],
                scores_ref[i, 128 * step : 128 * step + 64],
                scores_ref[i, 128 * step + 64 : 128 * step + 128],
                both[1][halo : halo + 64],
            )
            for chunk in range(4):
                row = i - 1 + step
                mark = chunk_marks[chunk][row : row + 1]
                bias = table_ref[step, chunk].reshape(64, 128) + mark
                shifted.append(parts[chunk][:, 0:128] * LOG2E + bias)
                grads.append(parts[chunk][:, 128:256])
        shifted, grads = jnp.concatenate(shifted, axis=0), jnp.concatenate(grads, axis=0)
        top = jnp.max(shifted, axis=0, keepdims=True)
        exponent = jnp.exp2(shifted - top)
        total = jnp.sum(exponent, axis=0, keepdims=True)
        weighted = jnp.sum(exponent * grads, axis=0, keepdims=True)
        inverse = 1.0 / total
        delta = weighted * inverse
        weights = exponent * (inverse * used[i : i + 1])
        grad_scores = weights * (grads - delta)
        sums_ref[steps[0] : steps[-1] + 1] += grad_scores.reshape(count, 4, 8, 8, 128)
        return weights.astype(jnp.bfloat16), grad_scores.astype(jnp.bfloat16)

    def gradients(i, weights_low, grad_low):
        steps, first, count = window(i)
        shares = jnp.dot(
            jnp.concatenate([grad_low, weights_low], axis=1),
            qg_ref[256 * i : 256 * i + 256],
            preferred_element_type=jnp.float32,
        )
        low_ref[i, 0 : 256 * count] = grad_low
        for step in steps:
            at = 256 * (step - steps[0])
            j = i - 1 + step
            part = shares[at : at + 256]
            if not (step == 2 or i == 0):
                part = part + p_ref[j]
            if step == 0 or i == 7:
                out_inner_ref[j] = part[0:64].astype(jnp.bfloat16)
                own_ref[j] = part[64:192]
                out_outer_ref[j] = part[192:256].astype(jnp.bfloat16)
            else:
                p_ref[j] = part

    both = {i: products(i) for i in range(8)}
    pairs = [softmax(i, both[i]) for i in range(8)]
    for i in range(8):
        gradients(i, *pairs[i])
    contract_bias(sums_ref, skew_ref, bias_out_ref)


def main(occupied, table, qg, scores, blocks, inner, outer, col_count):
    halo = jax.ShapeDtypeStruct((8, 64, 128), jnp.bfloat16)
    return pl.pallas_call(
        main_kernel,
        out_shape=(
            jax.ShapeDtypeStruct((8, 768, 128), jnp.bfloat16),
            jax.ShapeDtypeStruct((64, 2048), jnp.bfloat16),
            jax.ShapeDtypeStruct((8, 128, 128), jnp.float32),
            halo,
            halo,
            jax.ShapeDtypeStruct((col_count, 1, 640), jnp.float32),
        ),
        in_specs=[VMEM_SPEC] * 7,
        out_specs=(VMEM_SPEC,) * 6,
        scratch_shapes=[
            pltpu.VMEM((3, 4, 8, 8, 128), jnp.float32),
            pltpu.VMEM((17, 4, 8, 128), jnp.float32),
            pltpu.VMEM((2048, 128), jnp.bfloat16),
            pltpu.VMEM((8, 256, 128), jnp.float32),
        ],
        compiler_params=pltpu.CompilerParams(vmem_limit_bytes=24 << 20),
        name="attention_backward",
    )(occupied, table, qg, scores, blocks, inner, outer)


def query_kernel(low_ref, kt_ref, dq_ref):
    for i in range(8):
        _, first, count = window(i)
        grad_query = jnp.dot(
            kt_ref[:, 256 * first : 256 * (first + count)],
            low_ref[i, 0 : 256 * count],
            preferred_element_type=jnp.float32,
        )
        dq_ref[i] = (grad_query * 0.125).astype(jnp.bfloat16)


def query_gradients(low, kt):
    return pl.pallas_call(
        query_kernel,
        out_shape=jax.ShapeDtypeStruct((8, 64, 128), jnp.bfloat16),
        in_specs=[VMEM_SPEC] * 2,
        out_specs=VMEM_SPEC,
        compiler_params=pltpu.CompilerParams(vmem_limit_bytes=8 << 20),
        name="query_gradients",
    )(low, kt)


def combine_kernel(dq_ref, own_ref, inner_ref, outer_ref, bias_ref, out_ref):
    summed = jnp.sum(bias_ref[...], axis=0)
    high = summed.astype(jnp.bfloat16).astype(jnp.float32)
    rest = summed - high
    middle = rest.astype(jnp.bfloat16).astype(jnp.float32)
    rows = [
        piece[:, 128 * k : 128 * k + 128]
        for piece in (high, middle, rest - middle)
        for k in range(5)
    ]
    rows.append(jnp.zeros((1, 128), jnp.float32))
    pieces = jnp.concatenate(rows, axis=0).astype(jnp.bfloat16)
    for i in range(8):
        out_ref[i, 0:64] = dq_ref[i]
        for at, ref in ((0, inner_ref), (64, outer_ref)):
            summed = own_ref[i, at : at + 64] + ref[i].astype(jnp.float32)
            out_ref[i, 64 + at : 128 + at] = summed.astype(jnp.bfloat16)
        out_ref[i, 192:208] = pieces


def combine(dq, own, inner, outer, bias):
    return pl.pallas_call(
        combine_kernel,
        out_shape=jax.ShapeDtypeStruct((8, 208, 128), jnp.bfloat16),
        in_specs=[VMEM_SPEC] * 5,
        out_specs=VMEM_SPEC,
        compiler_params=pltpu.CompilerParams(vmem_limit_bytes=8 << 20),
        name="combine",
    )(dq, own, inner, outer, bias)


def unpack_kernel(z_ref, gq_hbm, gk_hbm, gv_hbm, gb_ref, gq_ref, gk_ref, gv_ref, pieces_ref, sems):
    even_col_here = even_col()
    low = lanes_of((128, 128)) < 64
    copies = [
        pltpu.make_async_copy(source, target, sems.at[at])
        for at, (source, target) in enumerate(
            ((gq_ref, gq_hbm), (gk_ref, gk_hbm), (gv_ref, gv_hbm))
        )
    ]

    def load(head, first, last):
        return z_ref[head, first:last].astype(jnp.float32)

    def by_rows(block):
        inner, outer = block[0:64].reshape(8, 8, 128), block[64:128].reshape(8, 8, 128)
        left = jnp.where(even_col_here, outer, inner)
        right = jnp.where(even_col_here, inner, outer)
        return jnp.concatenate([left, right], axis=1)

    for pair in range(4):
        lanes = pl.ds(128 * pair, 128)
        both = jnp.concatenate([load(2 * pair, 0, 64), load(2 * pair + 1, 0, 64)], axis=0)
        gq_ref[:, :, lanes] = jnp.transpose(both).reshape(8, 16, 128).astype(jnp.bfloat16)
    copies[0].start()
    for pair in range(4):
        lanes = pl.ds(128 * pair, 128)
        key = jnp.where(
            low, load(2 * pair, 64, 192), swap_halves(load(2 * pair + 1, 64, 192))
        )
        gk_ref[:, :, lanes] = by_rows(key).astype(jnp.bfloat16)
    copies[1].start()
    for pair in range(4):
        lanes = pl.ds(128 * pair, 128)
        value = jnp.where(
            low, swap_halves(load(2 * pair, 64, 192)), load(2 * pair + 1, 64, 192)
        )
        gv_ref[:, :, lanes] = by_rows(value).astype(jnp.bfloat16)
    copies[2].start()
    for head in range(8):
        pieces_ref[head] = load(head, 192, 208)
    for a in range(17):
        k = a // 4
        row = pieces_ref[:, k, :] + pieces_ref[:, k + 5, :] + pieces_ref[:, k + 10, :]
        if a % 4:
            row = pltpu.roll(row, 128 - 32 * (a % 4), 1)
        gb_ref[a] = row[:, 0:17]
    for copy in copies:
        copy.wait()


def unpack(blocks):
    token = jax.ShapeDtypeStruct((8, 16, 512), jnp.bfloat16)
    return pl.pallas_call(
        unpack_kernel,
        out_shape=(token, token, token, jax.ShapeDtypeStruct((17, 8, 17), jnp.float32)),
        in_specs=[VMEM_SPEC],
        out_specs=(HBM_SPEC,) * 3 + (VMEM_SPEC,),
        scratch_shapes=[pltpu.VMEM((8, 16, 512), jnp.bfloat16)] * 3
        + [pltpu.VMEM((8, 16, 128), jnp.float32), pltpu.SemaphoreType.DMA((3,))],
        compiler_params=pltpu.CompilerParams(vmem_limit_bytes=8 << 20),
        name="unpack",
    )(blocks)


def shards(queries, keys, values, grad_out, rel_bias, occupied):
    col_count = lax.axis_size("col")
    within = [(i, i ^ 1) for i in range(col_count)]
    between = [(i, i - 1 if i % 2 == 0 else i + 1) for i in range(1, col_count - 1)]
    packed = pack(queries, keys, values, grad_out)
    blocks = lax.all_to_all(packed, "row", 0, 0)
    inner = lax.ppermute(blocks[:, 128:192], "col", within)
    outer = lax.ppermute(blocks[:, 192:256], "col", between)
    bias = jnp.transpose(rel_bias, (1, 0, 2))
    low, kt, own, out_inner, out_outer, bias_part = main(
        occupied, *own_scores(bias, blocks), blocks, inner, outer, col_count
    )
    dq = query_gradients(low, kt)
    outer_share = lax.ppermute(out_outer, "col", between)
    inner_share = lax.ppermute(out_inner, "col", within)
    bias_parts = lax.all_to_all(bias_part, "col", 0, 0)
    returned = lax.all_to_all(combine(dq, own, inner_share, outer_share, bias_parts), "row", 0, 0)
    grad_query, grad_key, grad_value, grad_bias = unpack(returned)
    return grad_query, grad_key, grad_value, jnp.transpose(grad_bias, (1, 0, 2))


def solution(mesh):
    token = P("row", "col", None)
    return jax.shard_map(
        shards,
        mesh=mesh,
        in_specs=(token, token, token, token, P(), P()),
        out_specs=(token, token, token, P()),
        check_vma=False,
    )
```
